32 devices in a mesh: fsdp: 8 (over y, x, core), tp: 4 (over z).
Axes of the slice: x: 2, y: 2, z: 4, core: 2. Of those that a mesh axis runs over, the one named last changes fastest.
Arguments:
- tokens: bfloat16 [8192, 2048], P(('fsdp', 'tp')), may hold values from -6 to 6
- segments: int32 [8, 1024], P('fsdp'), may hold values from 0 to 7, never falling along the last dimension, each value on 1 to 512 neighbouring positions
- prefix: int32 [8], P('fsdp'), may hold values from 0 to 512
- expert_ids: int32 [8192, 8], P('fsdp'), may hold values from 0 to 31, all different within a row
- first_gain: bfloat16 [2048], P('fsdp'), may hold values from 0.25 to 1.75
- query_weight: bfloat16 [2048, 4096], P('fsdp', 'tp'), may hold values from -0.125 to 0.125
- key_matrix: bfloat16 [2048, 512], P('fsdp', 'tp'), may hold values from -0.125 to 0.125
- value_matrix: bfloat16 [2048, 512], P('fsdp', 'tp'), may hold values from -0.125 to 0.125
- query_gain: bfloat16 [128], P('fsdp'), may hold values from 0.25 to 1.75
- key_gain: bfloat16 [128], P('fsdp'), may hold values from 0.25 to 1.75
- output_weight: bfloat16 [2048, 4096], P('fsdp', 'tp'), may hold values from -0.75 to 0.75
- second_gain: bfloat16 [2048], P('fsdp'), may hold values from 0.25 to 1.75
- router: bfloat16 [2048, 32], P('fsdp'), may hold values from -0.125 to 0.125
- gate_weight: bfloat16 [32, 768, 2048], P('fsdp', 'tp'), may hold values from -0.125 to 0.125
- up_weight: bfloat16 [32, 768, 2048], P('fsdp', 'tp'), may hold values from -0.125 to 0.125
- down_weight: bfloat16 [32, 768, 2048], P('fsdp', 'tp'), may hold values from -0.625 to 0.625
- cotangent: bfloat16 [8192, 2048], P(('fsdp', 'tp')), may hold values from -6 to 6
Outputs:
- output: bfloat16 [8192, 2048], P(('fsdp', 'tp'))
- input_grad: bfloat16 [8192, 2048], P(('fsdp', 'tp'))
- first_gain_grad: float32 [2048], P(('fsdp', 'tp'))
- query_weight_grad: float32 [2048, 4096], P('fsdp', 'tp')
- key_weight_grad: float32 [2048, 512], P('fsdp', 'tp')
- value_weight_grad: float32 [2048, 512], P('fsdp', 'tp')
- query_gain_grad: float32 [128], P(('fsdp', 'tp'))
- key_gain_grad: float32 [128], P(('fsdp', 'tp'))
- output_weight_grad: float32 [2048, 4096], P('fsdp', 'tp')
- second_gain_grad: float32 [2048], P(('fsdp', 'tp'))
- router_grad: float32 [2048, 32], P(('fsdp', 'tp'))
- gate_weight_grad: float32 [32, 768, 2048], P('fsdp', 'tp')
- up_weight_grad: float32 [32, 768, 2048], P('fsdp', 'tp')
- down_weight_grad: float32 [32, 768, 2048], P('fsdp', 'tp')
The draws below stay inside these ranges and needn't reach their ends.
Inputs may be any that keep to these rules, and one draw needn't show every extreme that they name: Each row of expert_ids names 8 different experts. `segments`: segment numbers never fall along a sequence.
All inputs are finite; a program needn't handle non-finite values.
Results may differ from the reference program's by a relative error of at most 0.035.
Values may be sent and summed in bfloat16 or wider, within the bound.
No kernel may reach another device: no remote copies, remote signals or barrier semaphores. Data moves between devices by JAX's collectives and lax.ppermute only.
A program may use at most 576 MiB of HBM per device.

```python
import math
import jax
import jax.numpy as jnp
import numpy as np
from jax import lax

MODEL_WIDTH = 2048
QUERY_HEADS = 32
KEY_VALUE_HEADS = 4
HEAD_SIZE = 128
FE = 768
TOPK = 8
SEQ = 1024
SEQS = 8
TOKENS = 8192
EXPERTS = 32
CAP = 288
N_TP = 4


def place_ends(entries, stream_key, low, largest):
    spot = [jax.random.randint(jax.random.fold_in(stream_key, axis), (), 0, length) for axis, length in enumerate(entries.shape)]
    widest = entries.shape.index(max(entries.shape))
    beside = spot[:widest] + [(spot[widest] + 1) % entries.shape[widest]] + spot[widest + 1:]
    return entries.at[tuple(spot)].set(low).at[tuple(beside)].set(largest)


def steps_of(key, extent, split, low, top_value):
    gain = 1.0
    for dim, shards_of in split:
        steps = jax.random.uniform(jax.random.fold_in(jax.random.fold_in(key, 6), dim), (shards_of,), jnp.float32, low / len(split), top_value / len(split))
        gain = gain * jnp.repeat(jnp.exp(steps), extent[dim] // shards_of).reshape((-1,) + (1,) * (len(extent) - 1 - dim))
    return gain


def picks_of(rng, rows, count, top, lift):
    ranking = jax.random.permutation(jax.random.fold_in(rng, 1), count)
    pull = ranking
    for power in range(3):
        pull = pull * pull // count
    pull = pull * lift // count
    chance = jax.random.randint(jax.random.fold_in(rng, 2), (rows, count), 0, 4096) + pull
    sure = jax.random.permutation(jax.random.fold_in(rng, 3), rows)[jnp.arange(count) % rows]
    chance = jnp.where(jnp.arange(rows)[:, None] == sure[None, :], 1 << 14, chance)
    score = chance * count + jnp.arange(count)
    return lax.top_k(score.astype(jnp.int32), top)[1].astype(jnp.int32)


def length_profile(count, total, most, slope):
    loads = [(1 << 20) // math.isqrt(standing ** slope) + 1 for standing in range(2, count + 1)]
    surplus, counts = total - most - (count - 1), [1] * (count - 1)
    while surplus > 0:
        candidates = [i for i in range(count - 1) if counts[i] < most]
        whole, budget = sum([loads[i] for i in candidates]), surplus
        for i in candidates:
            extra = min(most - counts[i], max(1, budget * loads[i] // whole), surplus)
            counts[i] = counts[i] + extra
            surplus = surplus - extra
    return np.array([most] + counts)


def ragged(rng, amount, total, bound, lean):
    if amount == 2:
        one = jax.random.randint(rng, (), max(1, total - bound), min(bound, total - 1) + 1)
        return jnp.stack([one, total - one])
    sizes = jnp.asarray(length_profile(amount, total, bound, lean), jnp.int32)
    pairs = (amount - 1) // 2
    giver, receiver = sizes[1:1 + 2 * pairs:2], sizes[2:2 + 2 * pairs:2]
    room = jnp.minimum(giver - 1, bound - receiver)
    shifted = jax.random.randint(jax.random.fold_in(rng, 1), (pairs,), 0, 1 << 20) % (room + 1)
    sizes = sizes.at[1:1 + 2 * pairs:2].set(giver - shifted).at[2:2 + 2 * pairs:2].set(receiver + shifted)
    return sizes[jax.random.permutation(jax.random.fold_in(rng, 2), amount)]


def scatter_about(rng, dims, spread, most, shards=(), kind=jnp.bfloat16):
    factor_of = steps_of(rng, dims, shards, -0.22, 0.18) if shards else 1.0
    drawn = jax.random.normal(rng, dims, jnp.float32) * spread * factor_of
    return jnp.minimum(jnp.maximum(drawn, -most), most).astype(kind)


def setup_inputs(seed: int = 0) -> dict:
    streams_of = jax.random.split(jax.random.key(seed), 18)
    tokens = scatter_about(streams_of[0], (TOKENS, MODEL_WIDTH), 1.0, 6.0, ((0, 32),))
    segments = jax.vmap(lambda own: jnp.searchsorted(jnp.cumsum(ragged(own, 8, SEQ, SEQ // 2, 2)), jnp.arange(SEQ), side="right"))(jax.random.split(streams_of[1], SEQS)).reshape((SEQS, SEQ)).astype(jnp.int32)
    prefix = place_ends(jax.random.randint(streams_of[2], (SEQS,), 0, SEQ // 2 + 1), jax.random.fold_in(streams_of[2], 1), 0, (SEQ // 2 + 1) - 1).astype(jnp.int32)
    expert_ids = picks_of(streams_of[3], TOKENS, EXPERTS, TOPK, 2048)
    first_gain = jnp.clip(1.0 + 0.15 * jax.random.normal(streams_of[4], (MODEL_WIDTH,), jnp.float32), 0.25, 1.75).astype(jnp.bfloat16)
    query_weight = scatter_about(streams_of[5], (MODEL_WIDTH, QUERY_HEADS * HEAD_SIZE), MODEL_WIDTH ** -0.5, 0.125, ((0, 8), (1, 4)))
    key_matrix = scatter_about(streams_of[6], (MODEL_WIDTH, KEY_VALUE_HEADS * HEAD_SIZE), MODEL_WIDTH ** -0.5, 0.125, ((0, 8), (1, 4)))
    value_matrix = scatter_about(streams_of[7], (MODEL_WIDTH, KEY_VALUE_HEADS * HEAD_SIZE), MODEL_WIDTH ** -0.5, 0.125, ((0, 8), (1, 4)))
    query_gain = jnp.clip(1.0 + 0.15 * jax.random.normal(streams_of[8], (HEAD_SIZE,), jnp.float32), 0.25, 1.75).astype(jnp.bfloat16)
    key_gain = jnp.clip(1.0 + 0.15 * jax.random.normal(streams_of[9], (HEAD_SIZE,), jnp.float32), 0.25, 1.75).astype(jnp.bfloat16)
    output_weight = scatter_about(streams_of[10], (MODEL_WIDTH, QUERY_HEADS * HEAD_SIZE), (QUERY_HEADS * HEAD_SIZE // 64) ** -0.5, 0.75, ((0, 8), (1, 4)))
    second_gain = jnp.clip(1.0 + 0.15 * jax.random.normal(streams_of[11], (MODEL_WIDTH,), jnp.float32), 0.25, 1.75).astype(jnp.bfloat16)
    router = scatter_about(streams_of[12], (MODEL_WIDTH, EXPERTS), MODEL_WIDTH ** -0.5, 0.125, ((0, 8),))
    gate_weight = scatter_about(streams_of[13], (EXPERTS, FE, MODEL_WIDTH), MODEL_WIDTH ** -0.5, 0.125, ((0, 8), (1, 4)))
    up_weight = scatter_about(streams_of[14], (EXPERTS, FE, MODEL_WIDTH), MODEL_WIDTH ** -0.5, 0.125, ((0, 8), (1, 4)))
    down_weight = scatter_about(streams_of[15], (EXPERTS, FE, MODEL_WIDTH), (FE // 8) ** -0.5, 0.625, ((0, 8), (1, 4)))
    cotangent = scatter_about(streams_of[16], (TOKENS, MODEL_WIDTH), 1.0, 6.0, ((0, 32),))
    return dict(tokens=tokens, segments=segments, prefix=prefix, expert_ids=expert_ids, first_gain=first_gain, query_weight=query_weight, key_matrix=key_matrix, value_matrix=value_matrix, query_gain=query_gain, key_gain=key_gain, output_weight=output_weight, second_gain=second_gain, router=router, gate_weight=gate_weight, up_weight=up_weight, down_weight=down_weight, cotangent=cotangent)


EPSILON = 1e-06
THETA = 1000000.0
NEG_BIG = -1e+30
HIGHEST = lax.Precision.HIGHEST

@jax.custom_vjp
def lowered_output(v):
    return lax.optimization_barrier(v.astype(jnp.bfloat16)).astype(jnp.float32)

@jax.custom_vjp
def lowered_gradient(v):
    return v

def low_keep(v):
    return (lowered_output(v), None)

def low_pass(kept, grad):
    return (grad,)

def back_keep(v):
    return (v, None)

def back_low(kept, grad):
    return (lowered_output(grad),)
lowered_output.defvjp(low_keep, low_pass)
lowered_gradient.defvjp(back_keep, back_low)

def dense_output(activations, matrix):
    return jnp.dot(activations, matrix, precision=HIGHEST, preferred_element_type=jnp.float32)

def rms_norm(values, gain_vec):
    return values * lax.rsqrt(lax.optimization_barrier(jnp.mean(values * values, axis=-1, keepdims=True)) + EPSILON) * gain_vec

def rope_tables(segment_row):
    length_total = segment_row.shape[0]
    token_index = jnp.arange(length_total, dtype=jnp.int32)
    change = jnp.concatenate([jnp.ones((1,), jnp.int32), (segment_row[1:] != segment_row[:-1]).astype(jnp.int32)])
    doc_start = lax.cummax(token_index * change, axis=0)
    position = (token_index - doc_start).astype(jnp.float32)
    half_dim = HEAD_SIZE // 2
    inverse = THETA ** (-(jnp.arange(half_dim, dtype=jnp.float32) * 2.0) / HEAD_SIZE)
    angles = position[:, None] * inverse[None, :]
    angles = jnp.concatenate([angles, angles], axis=1)
    return (jnp.cos(angles)[:, None, :], jnp.sin(angles)[:, None, :])

def rotate(values, cos_table, sin_table):
    half_dim = values.shape[-1] // 2
    turned = jnp.concatenate([-values[..., half_dim:], values[..., :half_dim]], axis=-1)
    return values * cos_table + turned * sin_table

def block_mask(segment_row, prefix_len, block_begin, block_row_span):
    length_total = segment_row.shape[0]
    query_pos = block_begin + jnp.arange(block_row_span, dtype=jnp.int32)
    key_pos = jnp.arange(length_total, dtype=jnp.int32)
    query_seg = lax.dynamic_slice_in_dim(segment_row, block_begin, block_row_span, 0)
    same_doc = query_seg[:, None] == segment_row[None, :]
    allowed = (key_pos[None, :] <= query_pos[:, None]) | (key_pos[None, :] < prefix_len)
    return same_doc & allowed

def attention(query_head_rows, key_heads, value_head_rows, segment_row, prefix_len):
    length_total = query_head_rows.shape[0]
    block_row_span = min(512, length_total)
    starts = jnp.arange(length_total // block_row_span, dtype=jnp.int32) * block_row_span

    def one_block(block_begin):
        query_block_rows = lax.dynamic_slice_in_dim(query_head_rows, block_begin, block_row_span, 0).reshape(block_row_span, KEY_VALUE_HEADS, QUERY_HEADS // KEY_VALUE_HEADS, HEAD_SIZE)
        scores = lowered_gradient(jnp.einsum('bhgd,khd->hgbk', query_block_rows, key_heads, precision=HIGHEST, preferred_element_type=jnp.float32) * HEAD_SIZE ** (-0.5))
        visible = block_mask(segment_row, prefix_len, block_begin, block_row_span)
        probs = lowered_output(jax.nn.softmax(jnp.where(visible[None, None], scores, NEG_BIG), axis=-1))
        mixed_rows = jnp.einsum('hgbk,khd->bhgd', probs, value_head_rows, precision=HIGHEST, preferred_element_type=jnp.float32)
        return mixed_rows.reshape(block_row_span, QUERY_HEADS * HEAD_SIZE)
    return lax.map(jax.checkpoint(one_block), starts).reshape(length_total, QUERY_HEADS * HEAD_SIZE)

def expert_mix(normed_two, choice_row, router, gate_weight, up_weight, down_weight):
    length_total = normed_two.shape[0]
    experts = router.shape[1]
    logits = lowered_gradient(dense_output(normed_two, router))
    chosen_mask = choice_row[:, :, None] == jnp.arange(experts, dtype=jnp.int32)[None, None, :]
    chosen = lax.optimization_barrier(jnp.sum(jnp.where(chosen_mask, logits[:, None, :], 0.0), axis=-1))
    gate_probs = jax.nn.softmax(chosen, axis=-1)
    per_token = lax.optimization_barrier(jnp.sum(chosen_mask.astype(jnp.int32), axis=1, dtype=jnp.int32))
    earlier = (jnp.cumsum(per_token, axis=0, dtype=jnp.int32) - per_token).astype(jnp.int32)
    slot_pos = lax.optimization_barrier(jnp.sum(jnp.where(chosen_mask, earlier[:, None, :], 0), axis=-1, dtype=jnp.int32))
    in_capacity = slot_pos < CAP
    empty_slot = experts * CAP
    slot_index = jnp.where(in_capacity, choice_row * CAP + slot_pos, empty_slot).astype(jnp.int32)
    token_index = jnp.broadcast_to(jnp.arange(length_total, dtype=jnp.int32)[:, None], choice_row.shape)
    slot_token = jnp.full((empty_slot,), length_total, jnp.int32).at[slot_index.reshape(-1)].set(token_index.reshape(-1), mode='drop')
    padded = jnp.concatenate([normed_two, jnp.zeros((1, normed_two.shape[1]), jnp.float32)], axis=0)
    dispatched = padded[slot_token].reshape(experts, CAP, normed_two.shape[1])
    unit_count = FE // N_TP
    total_out = jnp.zeros(dispatched.shape, jnp.float32)
    for tp_part in range(N_TP):
        first_unit = tp_part * unit_count
        last_unit = first_unit + unit_count
        rows_in = lowered_gradient(dispatched)
        gate_pre = lowered_gradient(jnp.einsum('ecd,efd->ecf', rows_in, gate_weight[:, first_unit:last_unit, :], precision=HIGHEST, preferred_element_type=jnp.float32))
        up_pre = lowered_gradient(jnp.einsum('ecd,efd->ecf', rows_in, up_weight[:, first_unit:last_unit, :], precision=HIGHEST, preferred_element_type=jnp.float32))
        hidden_act = lowered_output(jax.nn.silu(gate_pre) * up_pre)
        part_out = lowered_output(lowered_gradient(jnp.einsum('ecf,efd->ecd', hidden_act, down_weight[:, first_unit:last_unit, :], precision=HIGHEST, preferred_element_type=jnp.float32)))
        total_out = total_out + part_out
    flat_out = jnp.concatenate([total_out.reshape(empty_slot, -1), jnp.zeros((1, normed_two.shape[1]), jnp.float32)], axis=0)
    picked = flat_out[slot_index]
    return lax.optimization_barrier(jnp.sum(gate_probs[:, :, None] * picked, axis=1))

def layer_group(group_rows, segment_row, prefix_len, choice_row, params):
    first_gain, query_weight, key_matrix, value_matrix, query_gain, key_gain, output_weight, second_gain, router, gate_weight, up_weight, down_weight = params
    length_total = group_rows.shape[0]
    first_normed = lowered_output(rms_norm(group_rows, first_gain))
    query_pre = lowered_gradient(dense_output(first_normed, query_weight)).reshape(length_total, QUERY_HEADS, HEAD_SIZE)
    key_before_norm = lowered_gradient(dense_output(first_normed, key_matrix)).reshape(length_total, KEY_VALUE_HEADS, HEAD_SIZE)
    value_head_rows = lowered_output(lowered_gradient(dense_output(first_normed, value_matrix))).reshape(length_total, KEY_VALUE_HEADS, HEAD_SIZE)
    cos_table, sin_table = rope_tables(segment_row)
    query_head_rows = lowered_output(rotate(rms_norm(query_pre, query_gain), cos_table, sin_table))
    key_heads = lowered_output(rotate(rms_norm(key_before_norm, key_gain), cos_table, sin_table))
    mixed_rows = attention(query_head_rows, key_heads, value_head_rows, segment_row, prefix_len)
    attended = lowered_gradient(dense_output(lowered_output(lowered_gradient(mixed_rows)), output_weight.T))
    hidden = group_rows + attended
    normed_two = lowered_output(rms_norm(hidden, second_gain))
    return hidden + expert_mix(normed_two, choice_row, router, gate_weight, up_weight, down_weight)

def reference(tokens, segments, prefix, expert_ids, first_gain, query_weight, key_matrix, value_matrix, query_gain, key_gain, output_weight, second_gain, router, gate_weight, up_weight, down_weight, cotangent):
    params = tuple((weight_item.astype(jnp.float32) for weight_item in (first_gain, query_weight, key_matrix, value_matrix, query_gain, key_gain, output_weight, second_gain, router, gate_weight, up_weight, down_weight)))
    group_tokens = tokens.astype(jnp.float32).reshape(SEQS, SEQ, MODEL_WIDTH)
    choice_groups = expert_ids.reshape(SEQS, SEQ, TOPK)

    def forward(group_input, weight_set):

        def one_group(group_item):
            group_rows, segment_row, prefix_len, choice_row = group_item
            return layer_group(group_rows, segment_row, prefix_len, choice_row, weight_set)
        return lax.map(jax.checkpoint(one_group), (group_input, segments, prefix, choice_groups))
    result, pullback = jax.vjp(forward, group_tokens, params)
    input_grad, weight_grads = pullback(cotangent.astype(jnp.float32).reshape(SEQS, SEQ, MODEL_WIDTH))
    return (result.reshape(TOKENS, MODEL_WIDTH).astype(jnp.bfloat16), input_grad.reshape(TOKENS, MODEL_WIDTH).astype(jnp.bfloat16), weight_grads[0], weight_grads[1], weight_grads[2], weight_grads[3], weight_grads[4], weight_grads[5], weight_grads[6], weight_grads[7], weight_grads[8], weight_grads[9], weight_grads[10], weight_grads[11])
```

```python
import functools

import jax
import jax.numpy as jnp
from jax import lax
from jax.experimental import pallas as pl
from jax.experimental.pallas import tpu as pltpu
from jax.sharding import PartitionSpec as P

EPSILON = 1e-06
THETA = 1000000.0
NEG_BIG = -1e30


def rope_tables(segment_row, head_dim):
    length_total = segment_row.shape[0]
    token_index = jnp.arange(length_total, dtype=jnp.int32)
    change = jnp.concatenate(
        [jnp.ones((1,), jnp.int32), (segment_row[1:] != segment_row[:-1]).astype(jnp.int32)]
    )
    doc_start = lax.cummax(token_index * change, axis=0)
    position = (token_index - doc_start).astype(jnp.float32)
    half_dim = head_dim // 2
    inverse = THETA ** (-(jnp.arange(half_dim, dtype=jnp.float32) * 2.0) / head_dim)
    angles = position[:, None] * inverse[None, :]
    angles = jnp.concatenate([angles, angles], axis=1)
    return (jnp.cos(angles)[:, None, :], jnp.sin(angles)[:, None, :])


def rotate(values, cos_table, sin_table):
    half_dim = values.shape[-1] // 2
    turned = jnp.concatenate([-values[..., half_dim:], values[..., :half_dim]], axis=-1)
    return values * cos_table + turned * sin_table


def rotate_back(gradient, cos_table, sin_table):
    half_dim = gradient.shape[-1] // 2
    scaled = gradient * sin_table
    turned = jnp.concatenate([scaled[..., half_dim:], -scaled[..., :half_dim]], axis=-1)
    return gradient * cos_table + turned


def norm_forward(values):
    inverse = lax.rsqrt(jnp.mean(values * values, axis=-1, keepdims=True) + EPSILON)
    return (values * inverse, inverse)


def norm_back(gradient, scaled, inverse, gain_vec):
    weighted = gradient * gain_vec
    return inverse * (weighted - scaled * jnp.mean(weighted * scaled, axis=-1, keepdims=True))


def block_mask(segment_row, token_pos, prefix_len, block_begin, block_row_span):
    query_pos = lax.dynamic_slice_in_dim(token_pos, block_begin, block_row_span, 0)
    key_pos = token_pos
    query_seg = lax.dynamic_slice_in_dim(segment_row, block_begin, block_row_span, 0)
    same_doc = query_seg[:, None] == segment_row[None, :]
    allowed = (key_pos[None, :] <= query_pos[:, None]) | (key_pos[None, :] < prefix_len)
    return same_doc & allowed


def block_scores(
    block_begin,
    query_head_rows,
    key_heads,
    segment_row,
    token_pos,
    prefix_len,
    block_row_span,
    score_scale,
):
    kv_count = key_heads.shape[1]
    head_dim = key_heads.shape[2]
    query_block_rows = lax.dynamic_slice_in_dim(
        query_head_rows, block_begin, block_row_span, 0
    ).reshape(block_row_span, kv_count, -1, head_dim)
    scores = (
        jnp.einsum(
            "bhgd,khd->hgbk", query_block_rows, key_heads, preferred_element_type=jnp.float32
        )
        * score_scale
    )
    visible = block_mask(segment_row, token_pos, prefix_len, block_begin, block_row_span)
    return (query_block_rows, jnp.where(visible[None, None], scores, NEG_BIG))


def forward_block(
    block_begin,
    query_head_rows,
    key_heads,
    value_head_rows,
    segment_row,
    token_pos,
    prefix_len,
    block_row_span,
    score_scale,
):
    query_block_rows, scores = block_scores(
        block_begin,
        query_head_rows,
        key_heads,
        segment_row,
        token_pos,
        prefix_len,
        block_row_span,
        score_scale,
    )
    top_score = jnp.max(scores, axis=-1, keepdims=True)
    log_total = top_score + jnp.log(jnp.sum(jnp.exp(scores - top_score), axis=-1, keepdims=True))
    probs_low = jnp.exp(scores - log_total).astype(jnp.bfloat16)
    mixed_rows = jnp.einsum(
        "hgbk,khd->bhgd", probs_low, value_head_rows, preferred_element_type=jnp.float32
    )
    return (mixed_rows.reshape(block_row_span, -1), log_total[..., 0])


def backward_block(
    carried,
    inputs,
    query_head_rows,
    key_heads,
    value_head_rows,
    mixed_grad,
    segment_row,
    token_pos,
    prefix_len,
    block_row_span,
    score_scale,
):
    key_acc, value_acc = carried
    block_begin, log_total = inputs
    kv_count = key_heads.shape[1]
    head_dim = key_heads.shape[2]
    query_block_rows, scores = block_scores(
        block_begin,
        query_head_rows,
        key_heads,
        segment_row,
        token_pos,
        prefix_len,
        block_row_span,
        score_scale,
    )
    grad_block = lax.dynamic_slice_in_dim(mixed_grad, block_begin, block_row_span, 0).reshape(
        block_row_span, kv_count, -1, head_dim
    )
    probs = jnp.exp(scores - log_total[..., None])
    prob_grad = jnp.einsum(
        "bhgd,khd->hgbk", grad_block, value_head_rows, preferred_element_type=jnp.float32
    )
    score_grad = (probs * (prob_grad - jnp.sum(probs * prob_grad, axis=-1, keepdims=True))).astype(
        jnp.bfloat16
    )
    query_grad = (
        jnp.einsum("hgbk,khd->bhgd", score_grad, key_heads, preferred_element_type=jnp.float32)
        * score_scale
    )
    key_acc = (
        key_acc
        + jnp.einsum(
            "hgbk,bhgd->khd", score_grad, query_block_rows, preferred_element_type=jnp.float32
        )
        * score_scale
    )
    value_acc = value_acc + jnp.einsum(
        "hgbk,bhgd->khd", probs.astype(jnp.bfloat16), grad_block, preferred_element_type=jnp.float32
    )
    return ((key_acc, value_acc), query_grad.reshape(block_row_span, -1, head_dim))


def to_experts(buffer):
    return lax.all_to_all(buffer, "fsdp", split_axis=0, concat_axis=2, tiled=True)[0]


def collect_whole(values):
    returned = lax.all_to_all(values[None], "fsdp", split_axis=2, concat_axis=0, tiled=True)
    return returned.reshape(-1, values.shape[2])


def expert_forward(pieces):
    rows_in, gate_mat, up_mat, down_mat = pieces
    unit_count = gate_mat.shape[0]
    both_pre = jnp.einsum(
        "rd,fd->rf",
        rows_in,
        jnp.concatenate([gate_mat, up_mat], axis=0),
        preferred_element_type=jnp.float32,
    )
    gate_pre = both_pre[:, :unit_count]
    up_pre = both_pre[:, unit_count:]
    activated = (jax.nn.silu(gate_pre) * up_pre).astype(jnp.bfloat16)
    expert_part = jnp.dot(activated, down_mat, preferred_element_type=jnp.float32).astype(
        jnp.bfloat16
    )
    return (gate_pre, up_pre, activated, expert_part)


def expert_backward(pieces):
    rows_in, grad_in, gate_pre, up_pre, activated, gate_mat, up_mat, down_mat = pieces
    unit_count = gate_mat.shape[0]
    act_grad = jnp.einsum("rd,fd->rf", grad_in, down_mat, preferred_element_type=jnp.float32)
    down_grad = jnp.einsum("rf,rd->fd", activated, grad_in, preferred_element_type=jnp.float32)
    sigmoid_gate = jax.nn.sigmoid(gate_pre)
    gate_grad = (act_grad * up_pre * sigmoid_gate * (1.0 + gate_pre * (1.0 - sigmoid_gate))).astype(
        jnp.bfloat16
    )
    up_grad = (act_grad * gate_pre * sigmoid_gate).astype(jnp.bfloat16)
    both_grad = jnp.concatenate([gate_grad, up_grad], axis=1)
    both_wgrad = jnp.einsum("rf,rd->fd", both_grad, rows_in, preferred_element_type=jnp.float32)
    row_grad = jnp.einsum(
        "rf,fd->rd",
        both_grad,
        jnp.concatenate([gate_mat, up_mat], axis=0),
        preferred_element_type=jnp.float32,
    ).astype(jnp.bfloat16)
    return (row_grad, both_wgrad[:unit_count], both_wgrad[unit_count:], down_grad)


def exchanged(
    tokens,
    segments,
    prefix,
    expert_ids,
    first_gain,
    query_weight,
    key_matrix,
    value_matrix,
    query_gain,
    key_gain,
    output_weight,
    second_gain,
    router,
    gate_weight,
    up_weight,
    down_weight,
    cotangent,
):
    tp_count = lax.axis_size("tp")
    fsdp_count = lax.axis_size("fsdp")
    tp_rank = lax.axis_index("tp")
    (
        first_all,
        query_all,
        key_all,
        value_all,
        qgain_all,
        kgain_all,
        output_all,
        second_all,
        router_all,
    ) = (
        lax.all_gather(first_gain, "fsdp", axis=0, tiled=True),
        lax.all_gather(query_weight, "fsdp", axis=0, tiled=True),
        lax.all_gather(key_matrix, "fsdp", axis=0, tiled=True),
        lax.all_gather(value_matrix, "fsdp", axis=0, tiled=True),
        lax.all_gather(query_gain, "fsdp", axis=0, tiled=True),
        lax.all_gather(key_gain, "fsdp", axis=0, tiled=True),
        lax.all_gather(output_weight, "fsdp", axis=0, tiled=True),
        lax.all_gather(second_gain, "fsdp", axis=0, tiled=True),
        lax.all_gather(router, "fsdp", axis=0, tiled=True),
    )
    gain_one = first_all.astype(jnp.float32)
    gain_two = second_all.astype(jnp.float32)
    gain_query = qgain_all.astype(jnp.float32)
    gain_key = kgain_all.astype(jnp.float32)
    own_rows = tokens.shape[0]
    row_start = tp_rank * own_rows
    seq_rows = lax.all_gather(tokens, "tp", axis=0, tiled=True)
    seq_len = seq_rows.shape[0]
    model_dim = seq_rows.shape[1]
    head_dim = gain_query.shape[0]
    query_count = query_all.shape[1] // head_dim
    kv_count = key_all.shape[1] // head_dim
    score_scale = head_dim ** (-0.5)
    block_row_span = min(512, seq_len)
    block_count = seq_len // block_row_span
    segment_row = segments[0]
    prefix_len = prefix[0]
    token_pos = jnp.arange(seq_len, dtype=jnp.int32)
    cos_table, sin_table = rope_tables(segment_row, head_dim)
    input_float = seq_rows.astype(jnp.float32)
    input_hat, input_inverse = norm_forward(input_float)
    first_normed = (input_hat * gain_one).astype(jnp.bfloat16)
    query_pre = jnp.dot(first_normed, query_all, preferred_element_type=jnp.float32).reshape(
        seq_len, query_count, head_dim
    )
    key_before_norm = jnp.dot(first_normed, key_all, preferred_element_type=jnp.float32).reshape(
        seq_len, kv_count, head_dim
    )
    value_head_rows = (
        jnp.dot(first_normed, value_all, preferred_element_type=jnp.float32)
        .astype(jnp.bfloat16)
        .reshape(seq_len, kv_count, head_dim)
    )
    query_hat, query_inverse = norm_forward(query_pre)
    key_hat, key_inverse = norm_forward(key_before_norm)
    query_head_rows = rotate(query_hat * gain_query, cos_table, sin_table).astype(jnp.bfloat16)
    key_heads = rotate(key_hat * gain_key, cos_table, sin_table).astype(jnp.bfloat16)
    starts = jnp.arange(block_count, dtype=jnp.int32) * block_row_span
    mixed_rows, log_totals = lax.map(
        lambda block_begin: forward_block(
            block_begin,
            query_head_rows,
            key_heads,
            value_head_rows,
            segment_row,
            token_pos,
            prefix_len,
            block_row_span,
            score_scale,
        ),
        starts,
    )
    mixed_low = mixed_rows.reshape(seq_len, query_count * head_dim).astype(jnp.bfloat16)
    attended = lax.psum(
        jnp.einsum("sa,da->sd", mixed_low, output_all, preferred_element_type=jnp.float32).astype(
            jnp.bfloat16
        ),
        "tp",
    ).astype(jnp.float32)
    hidden = input_float + attended
    hidden_hat, hidden_inverse = norm_forward(hidden)
    normed_two = (hidden_hat * gain_two).astype(jnp.bfloat16)
    expert_total = router_all.shape[1]
    top_count = expert_ids.shape[1]
    capacity = (9 * top_count * seq_len + 8 * expert_total - 1) // (8 * expert_total)
    logits = jnp.dot(normed_two, router_all, preferred_element_type=jnp.float32)
    chosen_mask = expert_ids[:, :, None] == jnp.arange(expert_total, dtype=jnp.int32)[None, None, :]
    chosen = jnp.sum(jnp.where(chosen_mask, logits[:, None, :], 0.0), axis=-1)
    gate_probs = jax.nn.softmax(chosen, axis=-1)
    per_token = jnp.sum(chosen_mask.astype(jnp.int32), axis=1)
    earlier = jnp.cumsum(per_token, axis=0) - per_token
    slot_pos = jnp.sum(jnp.where(chosen_mask, earlier[:, None, :], 0), axis=-1)
    in_capacity = slot_pos < capacity
    empty_slot = expert_total * capacity
    slot_index = jnp.where(in_capacity, expert_ids * capacity + slot_pos, empty_slot)
    token_index = jnp.broadcast_to(jnp.arange(seq_len, dtype=jnp.int32)[:, None], expert_ids.shape)
    slot_token = (
        jnp.full((empty_slot,), seq_len, jnp.int32)
        .at[slot_index.reshape(-1)]
        .set(token_index.reshape(-1), mode="drop")
    )
    slot_gate = (
        jnp.zeros((empty_slot,), jnp.float32)
        .at[slot_index.reshape(-1)]
        .set(gate_probs.reshape(-1), mode="drop")
    )
    local_experts = gate_weight.shape[0]
    send_shape = (fsdp_count, local_experts, capacity, model_dim)
    zero_row = jnp.zeros((1, model_dim), jnp.bfloat16)
    zero_one = jnp.zeros((1,), jnp.float32)
    padded_two = jnp.concatenate([normed_two, zero_row], axis=0)
    rows_in = to_experts(padded_two[slot_token].reshape(send_shape))
    gate_pre, up_pre, activated, expert_part = lax.map(
        expert_forward, (rows_in, gate_weight, up_weight, down_weight)
    )
    returned = collect_whole(expert_part)
    expert_mix = jax.ops.segment_sum(
        returned.astype(jnp.float32) * slot_gate[:, None], slot_token, num_segments=seq_len + 1
    )[:seq_len]
    expert_own = lax.psum_scatter(
        expert_mix.astype(jnp.bfloat16), "tp", scatter_dimension=0, tiled=True
    ).astype(jnp.float32)
    hidden_own = lax.dynamic_slice_in_dim(hidden, row_start, own_rows, 0)
    output = (hidden_own + expert_own).astype(jnp.bfloat16)
    grad_rows = lax.all_gather(cotangent, "tp", axis=0, tiled=True)
    grad_float = grad_rows.astype(jnp.float32)
    grad_pad = jnp.concatenate([grad_rows, zero_row], axis=0)
    slot_rows = grad_pad[slot_token]
    slot_grad = (
        (slot_rows.astype(jnp.float32) * slot_gate[:, None])
        .astype(jnp.bfloat16)
        .reshape(send_shape)
    )
    grad_in = to_experts(slot_grad)
    row_grad, gate_wgrad, up_wgrad, down_wgrad = lax.map(
        expert_backward,
        (rows_in, grad_in, gate_pre, up_pre, activated, gate_weight, up_weight, down_weight),
    )
    back_rows = collect_whole(row_grad)
    expert_input_part = jax.ops.segment_sum(
        back_rows.astype(jnp.float32), slot_token, num_segments=seq_len + 1
    )[:seq_len]
    slot_dot = jnp.sum(slot_rows.astype(jnp.float32) * returned.astype(jnp.float32), axis=-1)
    prob_part = jnp.concatenate([slot_dot, zero_one], axis=0)[slot_index]
    expert_input_grad, prob_grad = (
        lax.psum(expert_input_part.astype(jnp.bfloat16), "tp").astype(jnp.float32),
        lax.psum(prob_part.astype(jnp.bfloat16), "tp").astype(jnp.float32),
    )
    chosen_grad = gate_probs * (prob_grad - jnp.sum(gate_probs * prob_grad, axis=-1, keepdims=True))
    logit_grad = jnp.sum(jnp.where(chosen_mask, chosen_grad[:, :, None], 0.0), axis=1).astype(
        jnp.bfloat16
    )
    normed_two_grad = expert_input_grad + jnp.einsum(
        "se,de->sd", logit_grad, router_all, preferred_element_type=jnp.float32
    )
    hidden_grad = grad_float + norm_back(normed_two_grad, hidden_hat, hidden_inverse, gain_two)
    second_part = jnp.sum(
        lax.dynamic_slice_in_dim(normed_two_grad * hidden_hat, row_start, own_rows, 0), axis=0
    )
    router_part = jnp.einsum(
        "sd,se->de",
        lax.dynamic_slice_in_dim(normed_two, row_start, own_rows, 0),
        lax.dynamic_slice_in_dim(logit_grad, row_start, own_rows, 0),
        preferred_element_type=jnp.float32,
    )
    attended_grad = hidden_grad.astype(jnp.bfloat16)
    output_wgrad = jnp.einsum(
        "sd,sa->da", attended_grad, mixed_low, preferred_element_type=jnp.float32
    )
    mixed_grad = jnp.dot(attended_grad, output_all, preferred_element_type=jnp.float32).astype(
        jnp.bfloat16
    )
    zero_heads = jnp.zeros((seq_len, kv_count, head_dim), jnp.float32)
    (key_turn_grad, value_grad), query_turn_grad = lax.scan(
        lambda carried, inputs: backward_block(
            carried,
            inputs,
            query_head_rows,
            key_heads,
            value_head_rows,
            mixed_grad,
            segment_row,
            token_pos,
            prefix_len,
            block_row_span,
            score_scale,
        ),
        (zero_heads, zero_heads),
        (starts, log_totals),
    )
    query_turn_grad = query_turn_grad.reshape(seq_len, query_count, head_dim)
    query_norm_grad = rotate_back(query_turn_grad, cos_table, sin_table)
    key_norm_grad = rotate_back(key_turn_grad, cos_table, sin_table)
    query_gain_part = jnp.sum(query_norm_grad * query_hat, axis=(0, 1))
    key_gain_part = jnp.sum(key_norm_grad * key_hat, axis=(0, 1))
    query_pre_grad = (
        norm_back(query_norm_grad, query_hat, query_inverse, gain_query)
        .astype(jnp.bfloat16)
        .reshape(seq_len, -1)
    )
    key_pre_grad = (
        norm_back(key_norm_grad, key_hat, key_inverse, gain_key)
        .astype(jnp.bfloat16)
        .reshape(seq_len, -1)
    )
    value_low = value_grad.astype(jnp.bfloat16).reshape(seq_len, -1)
    query_wgrad = jnp.einsum(
        "sd,sa->da", first_normed, query_pre_grad, preferred_element_type=jnp.float32
    )
    key_wgrad = jnp.einsum(
        "sd,sa->da", first_normed, key_pre_grad, preferred_element_type=jnp.float32
    )
    value_wgrad = jnp.einsum(
        "sd,sa->da", first_normed, value_low, preferred_element_type=jnp.float32
    )
    normed_one_grad = (
        jnp.einsum("sa,da->sd", query_pre_grad, query_all, preferred_element_type=jnp.float32)
        + jnp.einsum("sa,da->sd", key_pre_grad, key_all, preferred_element_type=jnp.float32)
        + jnp.einsum("sa,da->sd", value_low, value_all, preferred_element_type=jnp.float32)
    )
    first_part = jnp.sum(normed_one_grad * input_hat, axis=0)
    input_part = norm_back(normed_one_grad, input_hat, input_inverse, gain_one)
    input_sum, first_sum, qgain_sum, kgain_sum, second_sum, router_sum = (
        lax.psum_scatter(
            input_part.astype(jnp.bfloat16), "tp", scatter_dimension=0, tiled=True
        ).astype(jnp.float32),
        lax.psum_scatter(
            first_part.reshape(fsdp_count, tp_count, -1).astype(jnp.bfloat16),
            "tp",
            scatter_dimension=1,
            tiled=True,
        ).astype(jnp.float32),
        lax.psum_scatter(
            query_gain_part.reshape(fsdp_count, tp_count, -1).astype(jnp.bfloat16),
            "tp",
            scatter_dimension=1,
            tiled=True,
        ).astype(jnp.float32),
        lax.psum_scatter(
            key_gain_part.reshape(fsdp_count, tp_count, -1).astype(jnp.bfloat16),
            "tp",
            scatter_dimension=1,
            tiled=True,
        ).astype(jnp.float32),
        lax.psum_scatter(
            second_part.reshape(fsdp_count, tp_count, -1).astype(jnp.bfloat16),
            "tp",
            scatter_dimension=1,
            tiled=True,
        ).astype(jnp.float32),
        lax.psum_scatter(
            router_part.reshape(fsdp_count, tp_count, -1, expert_total).astype(jnp.bfloat16),
            "tp",
            scatter_dimension=1,
            tiled=True,
        ).astype(jnp.float32),
    )
    input_grad = (lax.dynamic_slice_in_dim(hidden_grad, row_start, own_rows, 0) + input_sum).astype(
        jnp.bfloat16
    )
    (
        query_wshard,
        key_wshard,
        value_wshard,
        output_wshard,
        first_shard,
        qgain_shard,
        kgain_shard,
        second_shard,
        router_shard,
    ) = (
        lax.psum_scatter(
            query_wgrad.astype(jnp.bfloat16), "fsdp", scatter_dimension=0, tiled=True
        ).astype(jnp.float32),
        lax.psum_scatter(
            key_wgrad.astype(jnp.bfloat16), "fsdp", scatter_dimension=0, tiled=True
        ).astype(jnp.float32),
        lax.psum_scatter(
            value_wgrad.astype(jnp.bfloat16), "fsdp", scatter_dimension=0, tiled=True
        ).astype(jnp.float32),
        lax.psum_scatter(
            output_wgrad.astype(jnp.bfloat16), "fsdp", scatter_dimension=0, tiled=True
        ).astype(jnp.float32),
        lax.psum_scatter(
            first_sum.astype(jnp.bfloat16), "fsdp", scatter_dimension=0, tiled=True
        ).astype(jnp.float32),
        lax.psum_scatter(
            qgain_sum.astype(jnp.bfloat16), "fsdp", scatter_dimension=0, tiled=True
        ).astype(jnp.float32),
        lax.psum_scatter(
            kgain_sum.astype(jnp.bfloat16), "fsdp", scatter_dimension=0, tiled=True
        ).astype(jnp.float32),
        lax.psum_scatter(
            second_sum.astype(jnp.bfloat16), "fsdp", scatter_dimension=0, tiled=True
        ).astype(jnp.float32),
        lax.psum_scatter(
            router_sum.astype(jnp.bfloat16), "fsdp", scatter_dimension=0, tiled=True
        ).astype(jnp.float32),
    )
    return (
        output,
        input_grad,
        first_shard.reshape(-1),
        query_wshard,
        key_wshard,
        value_wshard,
        qgain_shard.reshape(-1),
        kgain_shard.reshape(-1),
        output_wshard,
        second_shard.reshape(-1),
        router_shard.reshape(-1, expert_total),
        gate_wgrad,
        up_wgrad,
        down_wgrad,
    )


def partners(count, mask):
    return [(i, i ^ mask) for i in range(count)]


def swap(values, axis, mask):
    return lax.ppermute(values, axis, partners(lax.axis_size(axis), mask))


def xor_order(values, index, axis):
    count = values.shape[axis]
    bit = 1
    while bit < count:
        shape = values.shape
        split = values.reshape(shape[:axis] + (count // (2 * bit), 2, bit) + shape[axis + 1 :])
        flipped = jnp.flip(split, axis + 1).reshape(shape)
        values = jnp.where((index & bit) != 0, flipped, values)
        bit *= 2
    return values


def plane_gather(block, odd):
    side = swap(block, "fsdp", 2)
    above = swap(block, "fsdp", 4)
    corner = swap(side, "fsdp", 4) if odd else swap(above, "fsdp", 2)
    gathered = []
    for held in (block, side, above, corner):
        gathered += [held, swap(held, "fsdp", 1)]
    return gathered


def add_low(*terms):
    total = terms[0].astype(jnp.float32)
    for term in terms[1:]:
        total = total + term.astype(jnp.float32)
    return total


def plane_reduce(parts, odd):
    low = jnp.bfloat16
    own, side, above, corner = [
        add_low(parts[m], swap(parts[m + 1], "fsdp", 1)).astype(low) for m in (0, 2, 4, 6)
    ]
    if odd:
        side = add_low(side, swap(corner, "fsdp", 4)).astype(low)
    else:
        above = add_low(above, swap(corner, "fsdp", 2)).astype(low)
    return add_low(own, swap(side, "fsdp", 2), swap(above, "fsdp", 4)).astype(low)


def tp_gather(block):
    return [block] + [swap(block, "tp", r) for r in range(1, lax.axis_size("tp"))]


def tp_reduce(parts):
    return add_low(parts[0], *[swap(parts[r], "tp", r) for r in range(1, len(parts))])


def small_reduce(parts):
    parts = parts[0::2] + swap(parts[1::2], "fsdp", 1)
    parts = parts[0::2] + swap(parts[1::2], "fsdp", 2)
    parts = parts[0] + swap(parts[1], "fsdp", 4)
    parts = parts[0::2] + swap(parts[1::2], "tp", 1)
    return parts[0] + swap(parts[1], "tp", 2)


def turned_tables(position, head_dim):
    half_dim = head_dim // 2
    inverse = THETA ** (-(jnp.arange(half_dim, dtype=jnp.float32) * 2.0) / head_dim)
    angles = position.astype(jnp.float32)[:, None] * inverse[None, :]
    angles = jnp.concatenate([angles, angles], axis=1)
    return (jnp.cos(angles)[:, None, :], jnp.sin(angles)[:, None, :])


def dot_nn(a, b):
    return lax.dot_general(a, b, (((1,), (0,)), ((), ())), preferred_element_type=jnp.float32)

def dot_nt(a, b):
    return lax.dot_general(a, b, (((1,), (1,)), ((), ())), preferred_element_type=jnp.float32)

def expert_kernel(pair_count, local_experts, lane_pad, *refs):
    count = 2 * pair_count
    x_refs, refs = refs[:count], refs[count:]
    c_refs, refs = refs[:count], refs[count:]
    code_ref, router_ref, gate_ref, up_ref, down_ref = refs[:5]
    refs = refs[5:]
    row_refs, refs = refs[:count], refs[count:]
    out_refs, refs = refs[:count], refs[count:]
    mixed_ref, act_ref, xb, cb, rb, ob, prod, in_sem, out_sem = refs
    rows = x_refs[0].shape[0]
    span = 2 * rows
    hidden, width = gate_ref.shape
    per_expert = hidden // local_experts
    step = pl.program_id(0)
    slot = lax.rem(step, 2)

    def loads(index, at):
        for k in range(2):
            where = pl.ds(k * rows, rows)
            yield pltpu.make_async_copy(x_refs[index + k], xb.at[at, where], in_sem.at[at, 2 * k])
            yield pltpu.make_async_copy(c_refs[index + k], cb.at[at, where], in_sem.at[at, 2 * k + 1])

    def stores(index, at):
        for k in range(2):
            where = pl.ds(k * rows, rows)
            yield pltpu.make_async_copy(rb.at[at, where], row_refs[index + k], out_sem.at[at, 2 * k])
            yield pltpu.make_async_copy(ob.at[at, where], out_refs[index + k], out_sem.at[at, 2 * k + 1])

    def start_loads(which, at):
        for j in range(pair_count):
            @pl.when(which == j)
            def _(j=j):
                for copy in loads(2 * j, at):
                    copy.start()

    @pl.when(step == 0)
    def _():
        start_loads(step, 0)

    @pl.when(step + 1 < pair_count)
    def _():
        start_loads(step + 1, 1 - slot)

    for copy in loads(0, slot):
        copy.wait()

    logits = dot_nn(xb[slot], router_ref[...])
    code = code_ref[0].astype(jnp.float32)
    chosen = code > 0.5
    top = jnp.max(jnp.where(chosen, logits, -1e30), axis=1, keepdims=True)
    powers = jnp.where(chosen, jnp.exp(logits - top), 0.0)
    probs = powers / jnp.sum(powers, axis=1, keepdims=True)
    kept = jnp.where(code > 1.5, probs, 0.0)
    tile = min(256, hidden)

    def hidden_step(j, carry):
        at = pl.multiple_of(j * tile, tile)
        cols = pl.ds(at, tile)
        gate = dot_nt(xb[slot], gate_ref[cols, :])
        up = dot_nt(xb[slot], up_ref[cols, :])
        act_grad = dot_nt(cb[slot], down_ref[cols, :])
        column = at + lax.broadcasted_iota(jnp.int32, (1, tile), 1)
        weight = kept[:, 0:1]
        for e in range(1, local_experts):
            weight = jnp.where(column < e * per_expert, weight, kept[:, e : e + 1])
        sigmoid = 1.0 / (1.0 + jnp.exp(-gate))
        silu = gate * sigmoid
        act = silu * up
        act_grad = act_grad * weight
        act_ref[:, cols] = (act * weight).astype(jnp.bfloat16)
        prod[:, cols] = (act * act_grad).astype(jnp.bfloat16)
        mixed_ref[:, cols] = (act_grad * up * (sigmoid + silu * (1.0 - sigmoid))).astype(jnp.bfloat16)
        mixed_ref[:, pl.ds(pl.multiple_of(hidden + at, 128), tile)] = (act_grad * silu).astype(jnp.bfloat16)
        return carry

    lax.fori_loop(0, hidden // tile, hidden_step, 0)
    owner = lax.broadcasted_iota(jnp.int32, (hidden, lane_pad), 0)
    lane = lax.broadcasted_iota(jnp.int32, (hidden, lane_pad), 1) * per_expert
    member = jnp.where((owner >= lane) & (owner < lane + per_expert), 1.0, 0.0).astype(jnp.bfloat16)
    weighted = dot_nn(prod[...], member)
    total = jnp.sum(weighted, axis=1, keepdims=True)
    mixed_ref[:, 2 * hidden :] = (weighted - probs * total).astype(jnp.bfloat16)

    @pl.when(step >= 2)
    def _():
        for copy in stores(0, slot):
            copy.wait()

    out_tile = min(256, width)

    def width_step(j, carry):
        cols = pl.ds(pl.multiple_of(j * out_tile, out_tile), out_tile)
        row_grad = dot_nn(mixed_ref[:, :hidden], gate_ref[:, cols])
        row_grad = row_grad + dot_nn(mixed_ref[:, hidden : 2 * hidden], up_ref[:, cols])
        row_grad = row_grad + dot_nt(mixed_ref[:, 2 * hidden :], router_ref[cols, :])
        rb[slot, :, cols] = row_grad.astype(jnp.bfloat16)
        ob[slot, :, cols] = dot_nn(act_ref[...], down_ref[:, cols]).astype(jnp.bfloat16)
        return carry

    lax.fori_loop(0, width // out_tile, width_step, 0)
    for j in range(pair_count):
        @pl.when(step == j)
        def _(j=j):
            for copy in stores(2 * j, slot):
                copy.start()

    @pl.when(step == pair_count - 1)
    def _():
        for copy in stores(0, slot):
            copy.wait()
        if pair_count > 1:
            for copy in stores(0, 1 - slot):
                copy.wait()


def expert_call(xs, cs, code, router, gate_mat, up_mat, down_mat, local_experts):
    count = len(xs)
    pair_count = count // 2
    rows, width = xs[0].shape
    hidden = gate_mat.shape[0]
    lane_pad = router.shape[1]
    span = 2 * rows
    mixed_width = 2 * hidden + lane_pad
    any_spec = pl.BlockSpec(memory_space=pl.ANY)
    whole = lambda shape: pl.BlockSpec(shape, lambda i: (0, 0), pipeline_mode=pl.Buffered(1))
    block = jax.ShapeDtypeStruct((rows, width), jnp.bfloat16)
    flops = 2 * span * pair_count * (width * hidden * 6 + width * lane_pad * 2)
    results = pl.pallas_call(
        functools.partial(expert_kernel, pair_count, local_experts, lane_pad),
        grid=(pair_count,),
        out_shape=[block] * (2 * count)
        + [
            jax.ShapeDtypeStruct((span * pair_count, mixed_width), jnp.bfloat16),
            jax.ShapeDtypeStruct((span * pair_count, hidden), jnp.bfloat16),
        ],
        in_specs=[any_spec] * (2 * count)
        + [
            pl.BlockSpec((1, span, lane_pad), lambda i: (i, 0, 0)),
            whole((width, lane_pad)),
            whole((hidden, width)),
            whole((hidden, width)),
            whole((hidden, width)),
        ],
        out_specs=[any_spec] * (2 * count)
        + [
            pl.BlockSpec((span, mixed_width), lambda i: (i, 0)),
            pl.BlockSpec((span, hidden), lambda i: (i, 0)),
        ],
        scratch_shapes=[
            pltpu.VMEM((2, span, width), jnp.bfloat16),
            pltpu.VMEM((2, span, width), jnp.bfloat16),
            pltpu.VMEM((2, span, width), jnp.bfloat16),
            pltpu.VMEM((2, span, width), jnp.bfloat16),
            pltpu.VMEM((span, hidden), jnp.bfloat16),
            pltpu.SemaphoreType.DMA((2, 4)),
            pltpu.SemaphoreType.DMA((2, 4)),
        ],
        compiler_params=pltpu.CompilerParams(
            dimension_semantics=("arbitrary",), vmem_limit_bytes=60 * 1024 * 1024
        ),
        cost_estimate=pl.CostEstimate(
            flops=flops,
            bytes_accessed=count * rows * width * 8 + 6 * hidden * width,
            transcendentals=span * pair_count * hidden,
        ),
        name="experts",
    )(*xs, *cs, code, router, gate_mat, up_mat, down_mat)
    return results[:count], results[count : 2 * count], results[2 * count], results[2 * count + 1]


def gathered(
    tokens,
    segments,
    prefix,
    expert_ids,
    first_gain,
    query_weight,
    key_matrix,
    value_matrix,
    query_gain,
    key_gain,
    output_weight,
    second_gain,
    router,
    gate_weight,
    up_weight,
    down_weight,
    cotangent,
):
    low = jnp.bfloat16
    full = jnp.float32
    tp_count = lax.axis_size("tp")
    fsdp_count = lax.axis_size("fsdp")
    tp_rank = lax.axis_index("tp")
    fsdp_rank = lax.axis_index("fsdp")
    own_rows, model_dim = tokens.shape
    seq_len = own_rows * tp_count
    head_dim = fsdp_count * query_gain.shape[0]
    query_count = query_weight.shape[1] // head_dim
    kv_count = key_matrix.shape[1] // head_dim
    score_scale = head_dim ** (-0.5)
    local_experts, hidden_units = gate_weight.shape[:2]
    expert_total = fsdp_count * local_experts
    top_count = expert_ids.shape[1]
    capacity = (9 * top_count * seq_len + 8 * expert_total - 1) // (8 * expert_total)

    token_blocks = tp_gather(tokens)
    wide_shard = jnp.concatenate([query_weight, key_matrix, value_matrix], axis=1)
    wide_all = lax.all_gather(wide_shard, "fsdp", axis=0, tiled=True)
    gains = lax.all_gather(
        jnp.concatenate([first_gain, second_gain, query_gain, key_gain]), "fsdp", axis=0
    )
    gain_one = gains[:, : first_gain.shape[0]].reshape(-1).astype(full)
    gains = gains[:, first_gain.shape[0] :]
    gain_two = gains[:, : second_gain.shape[0]].reshape(-1).astype(full)
    gains = gains[:, second_gain.shape[0] :]
    gain_query = gains[:, : query_gain.shape[0]].reshape(-1).astype(full)
    gain_key = gains[:, query_gain.shape[0] :].reshape(-1).astype(full)
    router_all = lax.all_gather(router, "fsdp", axis=0, tiled=True)
    output_all = lax.all_gather(output_weight, "fsdp", axis=0, tiled=True)

    lanes = jnp.arange(expert_total, dtype=jnp.int32)
    picked = jnp.sum((expert_ids[:, :, None] == lanes[None, None, :]).astype(full), axis=1)
    order = jnp.arange(seq_len, dtype=jnp.int32)
    before = (order[None, :] < order[:, None]).astype(low)
    earlier = jnp.dot(before, picked.astype(low), preferred_element_type=full)
    code = (picked * (1.0 + (earlier < capacity).astype(full))).astype(low)
    code = xor_order(code.reshape(tp_count, own_rows, expert_total), tp_rank, 0)
    codes = jnp.swapaxes(code, 1, 2)[None]
    for mask in (1, 2, 4):
        codes = jnp.concatenate([codes, swap(codes, "fsdp", mask)], axis=0)
    shift = fsdp_rank * local_experts
    codes = jnp.concatenate([codes, codes], axis=2)
    codes = jnp.swapaxes(lax.dynamic_slice_in_dim(codes, shift, expert_total, 2), 2, 3)
    lane_pad = 128
    codes = jnp.pad(codes, ((0, 0), (0, 0), (0, 0), (0, lane_pad - expert_total)))
    router_near = jnp.concatenate([router_all, router_all], axis=1)
    router_near = lax.dynamic_slice_in_dim(router_near, shift, expert_total, 1)
    router_near = jnp.pad(router_near, ((0, 0), (0, lane_pad - expert_total)))

    cotangent_blocks = tp_gather(cotangent)
    cotangent_near = [plane_gather(b, r % 2 == 1) for r, b in enumerate(cotangent_blocks)]

    segment_row = xor_order(segments[0].reshape(tp_count, own_rows), tp_rank, 0).reshape(-1)
    token_pos = xor_order(order.reshape(tp_count, own_rows), tp_rank, 0).reshape(-1)
    prefix_len = prefix[0]
    doc_start = jnp.sum((segment_row[None, :] < segment_row[:, None]).astype(jnp.int32), axis=1)
    cos_table, sin_table = turned_tables(token_pos - doc_start, head_dim)

    seq_rows = jnp.concatenate(token_blocks, axis=0)
    input_hat, input_inverse = norm_forward(seq_rows.astype(full))
    first_normed = (input_hat * gain_one).astype(low)
    wide_pre = jnp.dot(first_normed, wide_all, preferred_element_type=full)
    query_cols = query_count * head_dim
    kv_cols = kv_count * head_dim
    query_pre = wide_pre[:, :query_cols].reshape(seq_len, query_count, head_dim)
    key_pre = wide_pre[:, query_cols : query_cols + kv_cols].reshape(seq_len, kv_count, head_dim)
    value_heads = wide_pre[:, query_cols + kv_cols :].astype(low).reshape(seq_len, kv_count, head_dim)
    query_hat, query_inverse = norm_forward(query_pre)
    key_hat, key_inverse = norm_forward(key_pre)
    query_heads = rotate(query_hat * gain_query, cos_table, sin_table).astype(low)
    key_heads = rotate(key_hat * gain_key, cos_table, sin_table).astype(low)
    span = min(512, seq_len)
    starts = jnp.arange(seq_len // span, dtype=jnp.int32) * span
    mixed_rows, log_totals = lax.map(
        lambda begin: forward_block(
            begin, query_heads, key_heads, value_heads, segment_row, token_pos, prefix_len, span, score_scale
        ),
        starts,
    )
    mixed_low = mixed_rows.reshape(seq_len, query_cols).astype(low)
    attended_part = jnp.einsum("sa,da->sd", mixed_low, output_all, preferred_element_type=full).astype(low)
    attended = tp_reduce([attended_part[r * own_rows : (r + 1) * own_rows] for r in range(tp_count)])
    hidden = tokens.astype(full) + attended
    hidden_hat, hidden_inverse = norm_forward(hidden)
    normed_two = (hidden_hat * gain_two).astype(low)

    normed_blocks = tp_gather(normed_two)
    normed_near = [plane_gather(b, r % 2 == 1) for r, b in enumerate(normed_blocks)]
    gate_mat = gate_weight.reshape(-1, model_dim)
    up_mat = up_weight.reshape(-1, model_dim)
    down_mat = down_weight.reshape(-1, model_dim)
    row_sums, out_sums, mixed_grads, act_gates = [], [], [], []
    for r in range(tp_count):
        code_r = codes[:, r].reshape(fsdp_count // 2, 2 * own_rows, lane_pad)
        row_parts, out_parts, mixed_grad, act_gate = expert_call(
            normed_near[r], cotangent_near[r], code_r, router_near, gate_mat, up_mat, down_mat, local_experts
        )
        row_sums.append(plane_reduce(row_parts, r % 2 == 1))
        out_sums.append(plane_reduce(out_parts, r % 2 == 1))
        mixed_grads.append(mixed_grad)
        act_gates.append(act_gate)
    normed_two_grad = tp_reduce(row_sums)
    output = (hidden + tp_reduce(out_sums)).astype(low)

    flat = lambda near: jnp.concatenate([b for blocks in near for b in blocks], axis=0)
    wide_grad = jnp.einsum(
        "tf,td->fd", jnp.concatenate(mixed_grads, axis=0), flat(normed_near), preferred_element_type=full
    )
    down_grad = jnp.einsum(
        "tf,td->fd", jnp.concatenate(act_gates, axis=0), flat(cotangent_near), preferred_element_type=full
    )
    flat_hidden = local_experts * hidden_units
    gate_wgrad = wide_grad[:flat_hidden].reshape(gate_weight.shape)
    up_wgrad = wide_grad[flat_hidden : 2 * flat_hidden].reshape(up_weight.shape)
    down_wgrad = down_grad.reshape(down_weight.shape)
    router_part = wide_grad[2 * flat_hidden : 2 * flat_hidden + expert_total]
    router_part = jnp.concatenate([router_part, router_part], axis=0)
    router_part = lax.dynamic_slice_in_dim(router_part, expert_total - shift, expert_total, 0).T

    hidden_grad = cotangent.astype(full) + norm_back(normed_two_grad, hidden_hat, hidden_inverse, gain_two)
    second_part = jnp.sum(normed_two_grad * hidden_hat, axis=0)
    attended_grad = jnp.concatenate(tp_gather(hidden_grad.astype(low)), axis=0)
    output_wgrad = jnp.einsum("sd,sa->da", attended_grad, mixed_low, preferred_element_type=full)
    mixed_grad = jnp.dot(attended_grad, output_all, preferred_element_type=full).astype(low)
    zero_heads = jnp.zeros((seq_len, kv_count, head_dim), full)
    (key_turn_grad, value_grad), query_turn_grad = lax.scan(
        lambda carried, inputs: backward_block(
            carried,
            inputs,
            query_heads,
            key_heads,
            value_heads,
            mixed_grad,
            segment_row,
            token_pos,
            prefix_len,
            span,
            score_scale,
        ),
        (zero_heads, zero_heads),
        (starts, log_totals),
    )
    query_turn_grad = query_turn_grad.reshape(seq_len, query_count, head_dim)
    query_norm_grad = rotate_back(query_turn_grad, cos_table, sin_table)
    key_norm_grad = rotate_back(key_turn_grad, cos_table, sin_table)
    query_gain_part = jnp.sum(query_norm_grad * query_hat, axis=(0, 1))
    key_gain_part = jnp.sum(key_norm_grad * key_hat, axis=(0, 1))
    query_pre_grad = norm_back(query_norm_grad, query_hat, query_inverse, gain_query).astype(low)
    key_pre_grad = norm_back(key_norm_grad, key_hat, key_inverse, gain_key).astype(low)
    wide_pre_grad = jnp.concatenate(
        [
            query_pre_grad.reshape(seq_len, -1),
            key_pre_grad.reshape(seq_len, -1),
            value_grad.astype(low).reshape(seq_len, -1),
        ],
        axis=1,
    )
    wide_wgrad = jnp.einsum("sd,sa->da", first_normed, wide_pre_grad, preferred_element_type=full)
    normed_one_part = jnp.einsum("sa,da->sd", wide_pre_grad, wide_all, preferred_element_type=full).astype(low)
    normed_one_grad = tp_reduce([normed_one_part[r * own_rows : (r + 1) * own_rows] for r in range(tp_count)])
    own_hat, own_inverse = norm_forward(tokens.astype(full))
    first_part = jnp.sum(normed_one_grad * own_hat, axis=0)
    input_grad = (hidden_grad + norm_back(normed_one_grad, own_hat, own_inverse, gain_one)).astype(low)

    sizes = []
    pieces = []
    for part in (first_part, second_part, query_gain_part, key_gain_part, router_part):
        part = part.reshape(fsdp_count, tp_count, -1)
        sizes.append(part.shape[2])
        pieces.append(part)
    packed = jnp.concatenate(pieces, axis=2)
    packed = small_reduce(xor_order(xor_order(packed, fsdp_rank, 0), tp_rank, 1))
    small = []
    begin = 0
    for size in sizes:
        small.append(packed[begin : begin + size])
        begin += size
    wide_wshard = lax.psum_scatter(wide_wgrad.astype(low), "fsdp", scatter_dimension=0, tiled=True).astype(full)
    output_wshard = lax.psum_scatter(
        output_wgrad.astype(low), "fsdp", scatter_dimension=0, tiled=True
    ).astype(full)
    return (
        output,
        input_grad,
        small[0],
        wide_wshard[:, :query_cols],
        wide_wshard[:, query_cols : query_cols + kv_cols],
        wide_wshard[:, query_cols + kv_cols :],
        small[2],
        small[3],
        output_wshard,
        small[1],
        small[4].reshape(-1, expert_total),
        gate_wgrad,
        up_wgrad,
        down_wgrad,
    )


def solution(mesh):
    placed = (
        P(("fsdp", "tp"), None),
        P("fsdp", None),
        P("fsdp"),
        P("fsdp", None),
        P("fsdp"),
        P("fsdp", "tp"),
        P("fsdp", "tp"),
        P("fsdp", "tp"),
        P("fsdp"),
        P("fsdp"),
        P("fsdp", "tp"),
        P("fsdp"),
        P("fsdp", None),
        P("fsdp", "tp", None),
        P("fsdp", "tp", None),
        P("fsdp", "tp", None),
        P(("fsdp", "tp"), None),
    )
    return jax.shard_map(
        gathered if mesh.shape["fsdp"] == 8 and mesh.shape["tp"] == 4 else exchanged,
        mesh=mesh,
        in_specs=placed,
        out_specs=(
            P(("fsdp", "tp"), None),
            P(("fsdp", "tp"), None),
            P(("fsdp", "tp")),
            P("fsdp", "tp"),
            P("fsdp", "tp"),
            P("fsdp", "tp"),
            P(("fsdp", "tp")),
            P(("fsdp", "tp")),
            P("fsdp", "tp"),
            P(("fsdp", "tp")),
            P(("fsdp", "tp"), None),
            P("fsdp", "tp", None),
            P("fsdp", "tp", None),
            P("fsdp", "tp", None),
        ),
        check_vma=False,
    )
```

```python
import functools

import jax
import jax.numpy as jnp
from jax import lax
from jax.experimental import pallas as pl
from jax.experimental.pallas import tpu as pltpu
from jax.sharding import PartitionSpec as P

EPSILON = 1e-06
THETA = 1000000.0
NEG_BIG = -1e30


def rope_tables(segment_row, head_dim):
    length_total = segment_row.shape[0]
    token_index = jnp.arange(length_total, dtype=jnp.int32)
    change = jnp.concatenate(
        [jnp.ones((1,), jnp.int32), (segment_row[1:] != segment_row[:-1]).astype(jnp.int32)]
    )
    doc_start = lax.cummax(token_index * change, axis=0)
    position = (token_index - doc_start).astype(jnp.float32)
    half_dim = head_dim // 2
    inverse = THETA ** (-(jnp.arange(half_dim, dtype=jnp.float32) * 2.0) / head_dim)
    angles = position[:, None] * inverse[None, :]
    angles = jnp.concatenate([angles, angles], axis=1)
    return (jnp.cos(angles)[:, None, :], jnp.sin(angles)[:, None, :])


def rotate(values, cos_table, sin_table):
    half_dim = values.shape[-1] // 2
    turned = jnp.concatenate([-values[..., half_dim:], values[..., :half_dim]], axis=-1)
    return values * cos_table + turned * sin_table


def rotate_back(gradient, cos_table, sin_table):
    half_dim = gradient.shape[-1] // 2
    scaled = gradient * sin_table
    turned = jnp.concatenate([scaled[..., half_dim:], -scaled[..., :half_dim]], axis=-1)
    return gradient * cos_table + turned


def norm_forward(values):
    inverse = lax.rsqrt(jnp.mean(values * values, axis=-1, keepdims=True) + EPSILON)
    return (values * inverse, inverse)


def norm_back(gradient, scaled, inverse, gain_vec):
    weighted = gradient * gain_vec
    return inverse * (weighted - scaled * jnp.mean(weighted * scaled, axis=-1, keepdims=True))


def block_mask(segment_row, token_pos, prefix_len, block_begin, block_row_span):
    query_pos = lax.dynamic_slice_in_dim(token_pos, block_begin, block_row_span, 0)
    key_pos = token_pos
    query_seg = lax.dynamic_slice_in_dim(segment_row, block_begin, block_row_span, 0)
    same_doc = query_seg[:, None] == segment_row[None, :]
    allowed = (key_pos[None, :] <= query_pos[:, None]) | (key_pos[None, :] < prefix_len)
    return same_doc & allowed


def block_scores(
    block_begin,
    query_head_rows,
    key_heads,
    segment_row,
    token_pos,
    prefix_len,
    block_row_span,
    score_scale,
):
    kv_count = key_heads.shape[1]
    head_dim = key_heads.shape[2]
    query_block_rows = lax.dynamic_slice_in_dim(
        query_head_rows, block_begin, block_row_span, 0
    ).reshape(block_row_span, kv_count, -1, head_dim)
    scores = (
        jnp.einsum(
            "bhgd,khd->hgbk", query_block_rows, key_heads, preferred_element_type=jnp.float32
        )
        * score_scale
    )
    visible = block_mask(segment_row, token_pos, prefix_len, block_begin, block_row_span)
    return (query_block_rows, jnp.where(visible[None, None], scores, NEG_BIG))


def forward_block(
    block_begin,
    query_head_rows,
    key_heads,
    value_head_rows,
    segment_row,
    token_pos,
    prefix_len,
    block_row_span,
    score_scale,
):
    query_block_rows, scores = block_scores(
        block_begin,
        query_head_rows,
        key_heads,
        segment_row,
        token_pos,
        prefix_len,
        block_row_span,
        score_scale,
    )
    top_score = jnp.max(scores, axis=-1, keepdims=True)
    log_total = top_score + jnp.log(jnp.sum(jnp.exp(scores - top_score), axis=-1, keepdims=True))
    probs_low = jnp.exp(scores - log_total).astype(jnp.bfloat16)
    mixed_rows = jnp.einsum(
        "hgbk,khd->bhgd", probs_low, value_head_rows, preferred_element_type=jnp.float32
    )
    return (mixed_rows.reshape(block_row_span, -1), log_total[..., 0])


def backward_block(
    carried,
    inputs,
    query_head_rows,
    key_heads,
    value_head_rows,
    mixed_grad,
    segment_row,
    token_pos,
    prefix_len,
    block_row_span,
    score_scale,
):
    key_acc, value_acc = carried
    block_begin, log_total = inputs
    kv_count = key_heads.shape[1]
    head_dim = key_heads.shape[2]
    query_block_rows, scores = block_scores(
        block_begin,
        query_head_rows,
        key_heads,
        segment_row,
        token_pos,
        prefix_len,
        block_row_span,
        score_scale,
    )
    grad_block = lax.dynamic_slice_in_dim(mixed_grad, block_begin, block_row_span, 0).reshape(
        block_row_span, kv_count, -1, head_dim
    )
    probs = jnp.exp(scores - log_total[..., None])
    prob_grad = jnp.einsum(
        "bhgd,khd->hgbk", grad_block, value_head_rows, preferred_element_type=jnp.float32
    )
    score_grad = (probs * (prob_grad - jnp.sum(probs * prob_grad, axis=-1, keepdims=True))).astype(
        jnp.bfloat16
    )
    query_grad = (
        jnp.einsum("hgbk,khd->bhgd", score_grad, key_heads, preferred_element_type=jnp.float32)
        * score_scale
    )
    key_acc = (
        key_acc
        + jnp.einsum(
            "hgbk,bhgd->khd", score_grad, query_block_rows, preferred_element_type=jnp.float32
        )
        * score_scale
    )
    value_acc = value_acc + jnp.einsum(
        "hgbk,bhgd->khd", probs.astype(jnp.bfloat16), grad_block, preferred_element_type=jnp.float32
    )
    return ((key_acc, value_acc), query_grad.reshape(block_row_span, -1, head_dim))


def to_experts(buffer):
    return lax.all_to_all(buffer, "fsdp", split_axis=0, concat_axis=2, tiled=True)[0]


def collect_whole(values):
    returned = lax.all_to_all(values[None], "fsdp", split_axis=2, concat_axis=0, tiled=True)
    return returned.reshape(-1, values.shape[2])


def expert_forward(pieces):
    rows_in, gate_mat, up_mat, down_mat = pieces
    unit_count = gate_mat.shape[0]
    both_pre = jnp.einsum(
        "rd,fd->rf",
        rows_in,
        jnp.concatenate([gate_mat, up_mat], axis=0),
        preferred_element_type=jnp.float32,
    )
    gate_pre = both_pre[:, :unit_count]
    up_pre = both_pre[:, unit_count:]
    activated = (jax.nn.silu(gate_pre) * up_pre).astype(jnp.bfloat16)
    expert_part = jnp.dot(activated, down_mat, preferred_element_type=jnp.float32).astype(
        jnp.bfloat16
    )
    return (gate_pre, up_pre, activated, expert_part)


def expert_backward(pieces):
    rows_in, grad_in, gate_pre, up_pre, activated, gate_mat, up_mat, down_mat = pieces
    unit_count = gate_mat.shape[0]
    act_grad = jnp.einsum("rd,fd->rf", grad_in, down_mat, preferred_element_type=jnp.float32)
    down_grad = jnp.einsum("rf,rd->fd", activated, grad_in, preferred_element_type=jnp.float32)
    sigmoid_gate = jax.nn.sigmoid(gate_pre)
    gate_grad = (act_grad * up_pre * sigmoid_gate * (1.0 + gate_pre * (1.0 - sigmoid_gate))).astype(
        jnp.bfloat16
    )
    up_grad = (act_grad * gate_pre * sigmoid_gate).astype(jnp.bfloat16)
    both_grad = jnp.concatenate([gate_grad, up_grad], axis=1)
    both_wgrad = jnp.einsum("rf,rd->fd", both_grad, rows_in, preferred_element_type=jnp.float32)
    row_grad = jnp.einsum(
        "rf,fd->rd",
        both_grad,
        jnp.concatenate([gate_mat, up_mat], axis=0),
        preferred_element_type=jnp.float32,
    ).astype(jnp.bfloat16)
    return (row_grad, both_wgrad[:unit_count], both_wgrad[unit_count:], down_grad)


def exchanged(
    tokens,
    segments,
    prefix,
    expert_ids,
    first_gain,
    query_weight,
    key_matrix,
    value_matrix,
    query_gain,
    key_gain,
    output_weight,
    second_gain,
    router,
    gate_weight,
    up_weight,
    down_weight,
    cotangent,
):
    tp_count = lax.axis_size("tp")
    fsdp_count = lax.axis_size("fsdp")
    tp_rank = lax.axis_index("tp")
    (
        first_all,
        query_all,
        key_all,
        value_all,
        qgain_all,
        kgain_all,
        output_all,
        second_all,
        router_all,
    ) = (
        lax.all_gather(first_gain, "fsdp", axis=0, tiled=True),
        lax.all_gather(query_weight, "fsdp", axis=0, tiled=True),
        lax.all_gather(key_matrix, "fsdp", axis=0, tiled=True),
        lax.all_gather(value_matrix, "fsdp", axis=0, tiled=True),
        lax.all_gather(query_gain, "fsdp", axis=0, tiled=True),
        lax.all_gather(key_gain, "fsdp", axis=0, tiled=True),
        lax.all_gather(output_weight, "fsdp", axis=0, tiled=True),
        lax.all_gather(second_gain, "fsdp", axis=0, tiled=True),
        lax.all_gather(router, "fsdp", axis=0, tiled=True),
    )
    gain_one = first_all.astype(jnp.float32)
    gain_two = second_all.astype(jnp.float32)
    gain_query = qgain_all.astype(jnp.float32)
    gain_key = kgain_all.astype(jnp.float32)
    own_rows = tokens.shape[0]
    row_start = tp_rank * own_rows
    seq_rows = lax.all_gather(tokens, "tp", axis=0, tiled=True)
    seq_len = seq_rows.shape[0]
    model_dim = seq_rows.shape[1]
    head_dim = gain_query.shape[0]
    query_count = query_all.shape[1] // head_dim
    kv_count = key_all.shape[1] // head_dim
    score_scale = head_dim ** (-0.5)
    block_row_span = min(512, seq_len)
    block_count = seq_len // block_row_span
    segment_row = segments[0]
    prefix_len = prefix[0]
    token_pos = jnp.arange(seq_len, dtype=jnp.int32)
    cos_table, sin_table = rope_tables(segment_row, head_dim)
    input_float = seq_rows.astype(jnp.float32)
    input_hat, input_inverse = norm_forward(input_float)
    first_normed = (input_hat * gain_one).astype(jnp.bfloat16)
    query_pre = jnp.dot(first_normed, query_all, preferred_element_type=jnp.float32).reshape(
        seq_len, query_count, head_dim
    )
    key_before_norm = jnp.dot(first_normed, key_all, preferred_element_type=jnp.float32).reshape(
        seq_len, kv_count, head_dim
    )
    value_head_rows = (
        jnp.dot(first_normed, value_all, preferred_element_type=jnp.float32)
        .astype(jnp.bfloat16)
        .reshape(seq_len, kv_count, head_dim)
    )
    query_hat, query_inverse = norm_forward(query_pre)
    key_hat, key_inverse = norm_forward(key_before_norm)
    query_head_rows = rotate(query_hat * gain_query, cos_table, sin_table).astype(jnp.bfloat16)
    key_heads = rotate(key_hat * gain_key, cos_table, sin_table).astype(jnp.bfloat16)
    starts = jnp.arange(block_count, dtype=jnp.int32) * block_row_span
    mixed_rows, log_totals = lax.map(
        lambda block_begin: forward_block(
            block_begin,
            query_head_rows,
            key_heads,
            value_head_rows,
            segment_row,
            token_pos,
            prefix_len,
            block_row_span,
            score_scale,
        ),
        starts,
    )
    mixed_low = mixed_rows.reshape(seq_len, query_count * head_dim).astype(jnp.bfloat16)
    attended = lax.psum(
        jnp.einsum("sa,da->sd", mixed_low, output_all, preferred_element_type=jnp.float32).astype(
            jnp.bfloat16
        ),
        "tp",
    ).astype(jnp.float32)
    hidden = input_float + attended
    hidden_hat, hidden_inverse = norm_forward(hidden)
    normed_two = (hidden_hat * gain_two).astype(jnp.bfloat16)
    expert_total = router_all.shape[1]
    top_count = expert_ids.shape[1]
    capacity = (9 * top_count * seq_len + 8 * expert_total - 1) // (8 * expert_total)
    logits = jnp.dot(normed_two, router_all, preferred_element_type=jnp.float32)
    chosen_mask = expert_ids[:, :, None] == jnp.arange(expert_total, dtype=jnp.int32)[None, None, :]
    chosen = jnp.sum(jnp.where(chosen_mask, logits[:, None, :], 0.0), axis=-1)
    gate_probs = jax.nn.softmax(chosen, axis=-1)
    per_token = jnp.sum(chosen_mask.astype(jnp.int32), axis=1)
    earlier = jnp.cumsum(per_token, axis=0) - per_token
    slot_pos = jnp.sum(jnp.where(chosen_mask, earlier[:, None, :], 0), axis=-1)
    in_capacity = slot_pos < capacity
    empty_slot = expert_total * capacity
    slot_index = jnp.where(in_capacity, expert_ids * capacity + slot_pos, empty_slot)
    token_index = jnp.broadcast_to(jnp.arange(seq_len, dtype=jnp.int32)[:, None], expert_ids.shape)
    slot_token = (
        jnp.full((empty_slot,), seq_len, jnp.int32)
        .at[slot_index.reshape(-1)]
        .set(token_index.reshape(-1), mode="drop")
    )
    slot_gate = (
        jnp.zeros((empty_slot,), jnp.float32)
        .at[slot_index.reshape(-1)]
        .set(gate_probs.reshape(-1), mode="drop")
    )
    local_experts = gate_weight.shape[0]
    send_shape = (fsdp_count, local_experts, capacity, model_dim)
    zero_row = jnp.zeros((1, model_dim), jnp.bfloat16)
    zero_one = jnp.zeros((1,), jnp.float32)
    padded_two = jnp.concatenate([normed_two, zero_row], axis=0)
    rows_in = to_experts(padded_two[slot_token].reshape(send_shape))
    gate_pre, up_pre, activated, expert_part = lax.map(
        expert_forward, (rows_in, gate_weight, up_weight, down_weight)
    )
    returned = collect_whole(expert_part)
    expert_mix = jax.ops.segment_sum(
        returned.astype(jnp.float32) * slot_gate[:, None], slot_token, num_segments=seq_len + 1
    )[:seq_len]
    expert_own = lax.psum_scatter(
        expert_mix.astype(jnp.bfloat16), "tp", scatter_dimension=0, tiled=True
    ).astype(jnp.float32)
    hidden_own = lax.dynamic_slice_in_dim(hidden, row_start, own_rows, 0)
    output = (hidden_own + expert_own).astype(jnp.bfloat16)
    grad_rows = lax.all_gather(cotangent, "tp", axis=0, tiled=True)
    grad_float = grad_rows.astype(jnp.float32)
    grad_pad = jnp.concatenate([grad_rows, zero_row], axis=0)
    slot_rows = grad_pad[slot_token]
    slot_grad = (
        (slot_rows.astype(jnp.float32) * slot_gate[:, None])
        .astype(jnp.bfloat16)
        .reshape(send_shape)
    )
    grad_in = to_experts(slot_grad)
    row_grad, gate_wgrad, up_wgrad, down_wgrad = lax.map(
        expert_backward,
        (rows_in, grad_in, gate_pre, up_pre, activated, gate_weight, up_weight, down_weight),
    )
    back_rows = collect_whole(row_grad)
    expert_input_part = jax.ops.segment_sum(
        back_rows.astype(jnp.float32), slot_token, num_segments=seq_len + 1
    )[:seq_len]
    slot_dot = jnp.sum(slot_rows.astype(jnp.float32) * returned.astype(jnp.float32), axis=-1)
    prob_part = jnp.concatenate([slot_dot, zero_one], axis=0)[slot_index]
    expert_input_grad, prob_grad = (
        lax.psum(expert_input_part.astype(jnp.bfloat16), "tp").astype(jnp.float32),
        lax.psum(prob_part.astype(jnp.bfloat16), "tp").astype(jnp.float32),
    )
    chosen_grad = gate_probs * (prob_grad - jnp.sum(gate_probs * prob_grad, axis=-1, keepdims=True))
    logit_grad = jnp.sum(jnp.where(chosen_mask, chosen_grad[:, :, None], 0.0), axis=1).astype(
        jnp.bfloat16
    )
    normed_two_grad = expert_input_grad + jnp.einsum(
        "se,de->sd", logit_grad, router_all, preferred_element_type=jnp.float32
    )
    hidden_grad = grad_float + norm_back(normed_two_grad, hidden_hat, hidden_inverse, gain_two)
    second_part = jnp.sum(
        lax.dynamic_slice_in_dim(normed_two_grad * hidden_hat, row_start, own_rows, 0), axis=0
    )
    router_part = jnp.einsum(
        "sd,se->de",
        lax.dynamic_slice_in_dim(normed_two, row_start, own_rows, 0),
        lax.dynamic_slice_in_dim(logit_grad, row_start, own_rows, 0),
        preferred_element_type=jnp.float32,
    )
    attended_grad = hidden_grad.astype(jnp.bfloat16)
    output_wgrad = jnp.einsum(
        "sd,sa->da", attended_grad, mixed_low, preferred_element_type=jnp.float32
    )
    mixed_grad = jnp.dot(attended_grad, output_all, preferred_element_type=jnp.float32).astype(
        jnp.bfloat16
    )
    zero_heads = jnp.zeros((seq_len, kv_count, head_dim), jnp.float32)
    (key_turn_grad, value_grad), query_turn_grad = lax.scan(
        lambda carried, inputs: backward_block(
            carried,
            inputs,
            query_head_rows,
            key_heads,
            value_head_rows,
            mixed_grad,
            segment_row,
            token_pos,
            prefix_len,
            block_row_span,
            score_scale,
        ),
        (zero_heads, zero_heads),
        (starts, log_totals),
    )
    query_turn_grad = query_turn_grad.reshape(seq_len, query_count, head_dim)
    query_norm_grad = rotate_back(query_turn_grad, cos_table, sin_table)
    key_norm_grad = rotate_back(key_turn_grad, cos_table, sin_table)
    query_gain_part = jnp.sum(query_norm_grad * query_hat, axis=(0, 1))
    key_gain_part = jnp.sum(key_norm_grad * key_hat, axis=(0, 1))
    query_pre_grad = (
        norm_back(query_norm_grad, query_hat, query_inverse, gain_query)
        .astype(jnp.bfloat16)
        .reshape(seq_len, -1)
    )
    key_pre_grad = (
        norm_back(key_norm_grad, key_hat, key_inverse, gain_key)
        .astype(jnp.bfloat16)
        .reshape(seq_len, -1)
    )
    value_low = value_grad.astype(jnp.bfloat16).reshape(seq_len, -1)
    query_wgrad = jnp.einsum(
        "sd,sa->da", first_normed, query_pre_grad, preferred_element_type=jnp.float32
    )
    key_wgrad = jnp.einsum(
        "sd,sa->da", first_normed, key_pre_grad, preferred_element_type=jnp.float32
    )
    value_wgrad = jnp.einsum(
        "sd,sa->da", first_normed, value_low, preferred_element_type=jnp.float32
    )
    normed_one_grad = (
        jnp.einsum("sa,da->sd", query_pre_grad, query_all, preferred_element_type=jnp.float32)
        + jnp.einsum("sa,da->sd", key_pre_grad, key_all, preferred_element_type=jnp.float32)
        + jnp.einsum("sa,da->sd", value_low, value_all, preferred_element_type=jnp.float32)
    )
    first_part = jnp.sum(normed_one_grad * input_hat, axis=0)
    input_part = norm_back(normed_one_grad, input_hat, input_inverse, gain_one)
    input_sum, first_sum, qgain_sum, kgain_sum, second_sum, router_sum = (
        lax.psum_scatter(
            input_part.astype(jnp.bfloat16), "tp", scatter_dimension=0, tiled=True
        ).astype(jnp.float32),
        lax.psum_scatter(
            first_part.reshape(fsdp_count, tp_count, -1).astype(jnp.bfloat16),
            "tp",
            scatter_dimension=1,
            tiled=True,
        ).astype(jnp.float32),
        lax.psum_scatter(
            query_gain_part.reshape(fsdp_count, tp_count, -1).astype(jnp.bfloat16),
            "tp",
            scatter_dimension=1,
            tiled=True,
        ).astype(jnp.float32),
        lax.psum_scatter(
            key_gain_part.reshape(fsdp_count, tp_count, -1).astype(jnp.bfloat16),
            "tp",
            scatter_dimension=1,
            tiled=True,
        ).astype(jnp.float32),
        lax.psum_scatter(
            second_part.reshape(fsdp_count, tp_count, -1).astype(jnp.bfloat16),
            "tp",
            scatter_dimension=1,
            tiled=True,
        ).astype(jnp.float32),
        lax.psum_scatter(
            router_part.reshape(fsdp_count, tp_count, -1, expert_total).astype(jnp.bfloat16),
            "tp",
            scatter_dimension=1,
            tiled=True,
        ).astype(jnp.float32),
    )
    input_grad = (lax.dynamic_slice_in_dim(hidden_grad, row_start, own_rows, 0) + input_sum).astype(
        jnp.bfloat16
    )
    (
        query_wshard,
        key_wshard,
        value_wshard,
        output_wshard,
        first_shard,
        qgain_shard,
        kgain_shard,
        second_shard,
        router_shard,
    ) = (
        lax.psum_scatter(
            query_wgrad.astype(jnp.bfloat16), "fsdp", scatter_dimension=0, tiled=True
        ).astype(jnp.float32),
        lax.psum_scatter(
            key_wgrad.astype(jnp.bfloat16), "fsdp", scatter_dimension=0, tiled=True
        ).astype(jnp.float32),
        lax.psum_scatter(
            value_wgrad.astype(jnp.bfloat16), "fsdp", scatter_dimension=0, tiled=True
        ).astype(jnp.float32),
        lax.psum_scatter(
            output_wgrad.astype(jnp.bfloat16), "fsdp", scatter_dimension=0, tiled=True
        ).astype(jnp.float32),
        lax.psum_scatter(
            first_sum.astype(jnp.bfloat16), "fsdp", scatter_dimension=0, tiled=True
        ).astype(jnp.float32),
        lax.psum_scatter(
            qgain_sum.astype(jnp.bfloat16), "fsdp", scatter_dimension=0, tiled=True
        ).astype(jnp.float32),
        lax.psum_scatter(
            kgain_sum.astype(jnp.bfloat16), "fsdp", scatter_dimension=0, tiled=True
        ).astype(jnp.float32),
        lax.psum_scatter(
            second_sum.astype(jnp.bfloat16), "fsdp", scatter_dimension=0, tiled=True
        ).astype(jnp.float32),
        lax.psum_scatter(
            router_sum.astype(jnp.bfloat16), "fsdp", scatter_dimension=0, tiled=True
        ).astype(jnp.float32),
    )
    return (
        output,
        input_grad,
        first_shard.reshape(-1),
        query_wshard,
        key_wshard,
        value_wshard,
        qgain_shard.reshape(-1),
        kgain_shard.reshape(-1),
        output_wshard,
        second_shard.reshape(-1),
        router_shard.reshape(-1, expert_total),
        gate_wgrad,
        up_wgrad,
        down_wgrad,
    )


def partners(count, mask):
    return [(i, i ^ mask) for i in range(count)]


def swap(values, axis, mask):
    return lax.ppermute(values, axis, partners(lax.axis_size(axis), mask))


def xor_order(values, index, axis):
    count = values.shape[axis]
    bit = 1
    while bit < count:
        shape = values.shape
        split = values.reshape(shape[:axis] + (count // (2 * bit), 2, bit) + shape[axis + 1 :])
        flipped = jnp.flip(split, axis + 1).reshape(shape)
        values = jnp.where((index & bit) != 0, flipped, values)
        bit *= 2
    return values


def chip_groups():
    count = lax.axis_size("fsdp")
    return [list(range(core, count, 2)) for core in range(2)]


def exchange(parts):
    return lax.all_to_all(
        parts, "fsdp", split_axis=0, concat_axis=0, tiled=True, axis_index_groups=chip_groups()
    )


def plane_gather(block):
    return exchange(jnp.broadcast_to(block[None], (lax.axis_size("fsdp") // 2, *block.shape)))


def add_low(*terms):
    total = terms[0].astype(jnp.float32)
    for term in terms[1:]:
        total = total + term.astype(jnp.float32)
    return total


def plane_reduce(terms):
    low = jnp.bfloat16
    both = add_low(terms[0], swap(terms[1], "fsdp", 1)).astype(low)
    return jnp.sum(exchange(both).astype(jnp.float32), axis=0).astype(low)


def tp_gather(block):
    return [block] + [swap(block, "tp", r) for r in range(1, lax.axis_size("tp"))]


def tp_reduce(parts):
    return add_low(parts[0], *[swap(parts[r], "tp", r) for r in range(1, len(parts))])


def small_reduce(parts):
    parts = parts[0::2] + swap(parts[1::2], "fsdp", 1)
    parts = parts[0::2] + swap(parts[1::2], "fsdp", 2)
    parts = parts[0] + swap(parts[1], "fsdp", 4)
    parts = parts[0::2] + swap(parts[1::2], "tp", 1)
    return parts[0] + swap(parts[1], "tp", 2)


def turned_tables(position, head_dim):
    half_dim = head_dim // 2
    inverse = THETA ** (-(jnp.arange(half_dim, dtype=jnp.float32) * 2.0) / head_dim)
    angles = position.astype(jnp.float32)[:, None] * inverse[None, :]
    angles = jnp.concatenate([angles, angles], axis=1)
    return (jnp.cos(angles)[:, None, :], jnp.sin(angles)[:, None, :])

def dot_nn(a, b):
    return lax.dot_general(a, b, (((1,), (0,)), ((), ())), preferred_element_type=jnp.float32)


def dot_nt(a, b):
    return lax.dot_general(a, b, (((1,), (1,)), ((), ())), preferred_element_type=jnp.float32)


def expert_kernel(local_experts, kept_count, where_ref, *refs):
    x_refs, c_refs, code_refs = refs[0:2], refs[2:4], refs[4:6]
    router_ref, gate_ref, up_ref, down_ref = refs[6:10]
    refs = refs[10 + kept_count :]
    row_refs, out_refs, all_refs = refs[0:2], refs[2:4], refs[4:7]
    mixed_ref, act_ref, prod, sem = refs[7:]
    rows = x_refs[0].shape[1]
    hidden, width = gate_ref.shape
    lane_pad = router_ref.shape[0]
    per_expert = hidden // local_experts
    step = pl.program_id(0)
    core, block = where_ref[0], where_ref[1]

    def keep(which, k):
        source = (x_refs[k].at[0], mixed_ref.at[pl.ds(k * rows, rows)], act_ref.at[pl.ds(k * rows, rows)])[which]
        owner = 2 * step + (core if k == 0 else 1 - core)
        return pltpu.make_async_copy(source, all_refs[which].at[owner, block], sem.at[which, k])

    for k in range(2):
        keep(0, k).start()
    logits, codes = [], []
    for k in range(2):
        logits.append(dot_nt(x_refs[k][0], router_ref[...]))
        codes.append(code_refs[k][0, 0].astype(jnp.float32))
    logits = jnp.concatenate(logits, axis=0)
    code = jnp.concatenate(codes, axis=0)
    chosen = code > 0.5
    top = jnp.max(jnp.where(chosen, logits, -1e30), axis=1, keepdims=True)
    powers = jnp.where(chosen, jnp.exp(logits - top), 0.0)
    probs = powers / jnp.sum(powers, axis=1, keepdims=True)
    kept = jnp.where(code > 1.5, probs, 0.0)
    tile = min(256, hidden)

    def hidden_step(j, carry):
        at = pl.multiple_of(j * tile, tile)
        cols = pl.ds(at, tile)
        both = lambda sides, matrix: jnp.concatenate([dot_nt(sides[k][0], matrix) for k in range(2)], axis=0)
        gate = both(x_refs, gate_ref[cols, :])
        up = both(x_refs, up_ref[cols, :])
        act_grad = both(c_refs, down_ref[cols, :])
        column = at + lax.broadcasted_iota(jnp.int32, (1, tile), 1)
        weight = kept[:, 0:1]
        for e in range(1, local_experts):
            weight = jnp.where(column < e * per_expert, weight, kept[:, e : e + 1])
        sigmoid = 1.0 / (1.0 + jnp.exp(-gate))
        silu = gate * sigmoid
        act = silu * up
        act_grad = act_grad * weight
        act_ref[:, cols] = (act * weight).astype(jnp.bfloat16)
        prod[:, cols] = (act * act_grad).astype(jnp.bfloat16)
        mixed_ref[:, cols] = (act_grad * up * (sigmoid + silu * (1.0 - sigmoid))).astype(jnp.bfloat16)
        mixed_ref[:, pl.ds(pl.multiple_of(hidden + at, 128), tile)] = (act_grad * silu).astype(jnp.bfloat16)
        return carry

    lax.fori_loop(0, hidden // tile, hidden_step, 0)
    for k in range(2):
        keep(2, k).start()
    owner = lax.broadcasted_iota(jnp.int32, (hidden, lane_pad), 0)
    lane = lax.broadcasted_iota(jnp.int32, (hidden, lane_pad), 1) * per_expert
    member = jnp.where((owner >= lane) & (owner < lane + per_expert), 1.0, 0.0).astype(jnp.bfloat16)
    weighted = dot_nn(prod[...], member)
    total = jnp.sum(weighted, axis=1, keepdims=True)
    mixed_ref[:, 2 * hidden :] = (weighted - probs * total).astype(jnp.bfloat16)
    for k in range(2):
        keep(1, k).start()
    out_tile = min(256, width)

    def width_step(j, carry):
        cols = pl.ds(pl.multiple_of(j * out_tile, out_tile), out_tile)
        row_grad = dot_nn(mixed_ref[:, :hidden], gate_ref[:, cols])
        row_grad = row_grad + dot_nn(mixed_ref[:, hidden : 2 * hidden], up_ref[:, cols])
        row_grad = row_grad + dot_nn(mixed_ref[:, 2 * hidden :], router_ref[:, cols])
        row_grad = row_grad.astype(jnp.bfloat16)
        out = dot_nn(act_ref[...], down_ref[:, cols]).astype(jnp.bfloat16)
        for k in range(2):
            row_refs[k][0, :, cols] = row_grad[k * rows : (k + 1) * rows]
            out_refs[k][0, :, cols] = out[k * rows : (k + 1) * rows]
        return carry

    lax.fori_loop(0, width // out_tile, width_step, 0)
    for which in range(3):
        for k in range(2):
            keep(which, k).wait()


def expert_call(where, xs, cotangents, codes, router, gate_mat, up_mat, down_mat, local_experts, kept):
    chips, rows, width = xs[0].shape
    hidden = gate_mat.shape[0]
    lane_pad = router.shape[0]
    mixed_width = 2 * hidden + lane_pad
    blocks = cotangents.shape[:2]
    any_spec = pl.BlockSpec(memory_space=pl.ANY)
    whole = lambda shape: pl.BlockSpec(shape, lambda i, w: (0, 0), pipeline_mode=pl.Buffered(1))
    near = lambda: pl.BlockSpec((1, rows, width), lambda i, w: (i, 0, 0))
    mine = lambda last: pl.BlockSpec((1, 1, rows, last), lambda i, w: (2 * i + w[0], w[1], 0, 0))
    theirs = lambda last: pl.BlockSpec((1, 1, rows, last), lambda i, w: (2 * i + 1 - w[0], w[1], 0, 0))
    squeezed = lambda build: pl.BlockSpec((1, None, rows, width), build(width).index_map)
    term = jax.ShapeDtypeStruct((chips, rows, width), jnp.bfloat16)
    alls = [jax.ShapeDtypeStruct((*blocks, rows, last), jnp.bfloat16) for last in (width, mixed_width, hidden)]
    count = 2 * chips * rows
    results = pl.pallas_call(
        functools.partial(expert_kernel, local_experts, len(kept)),
        grid_spec=pltpu.PrefetchScalarGridSpec(
            num_scalar_prefetch=1,
            grid=(chips,),
            in_specs=[near(), near(), squeezed(mine), squeezed(theirs), mine(lane_pad), theirs(lane_pad)]
            + [whole((lane_pad, width))]
            + [whole((hidden, width))] * 3
            + [any_spec] * len(kept),
            out_specs=[near() for _ in range(4)] + [any_spec] * 3,
            scratch_shapes=[
                pltpu.VMEM((2 * rows, mixed_width), jnp.bfloat16),
                pltpu.VMEM((2 * rows, hidden), jnp.bfloat16),
                pltpu.VMEM((2 * rows, hidden), jnp.bfloat16),
                pltpu.SemaphoreType.DMA((3, 2)),
            ],
        ),
        out_shape=[term] * 4 + alls,
        input_output_aliases={11 + k: 4 + k for k in range(len(kept))},
        compiler_params=pltpu.CompilerParams(
            dimension_semantics=("arbitrary",), vmem_limit_bytes=60 * 1024 * 1024
        ),
        cost_estimate=pl.CostEstimate(
            flops=count * (12 * width * hidden + 4 * width * lane_pad),
            bytes_accessed=count * (10 * width + 6 * hidden) + 6 * hidden * width,
            transcendentals=count * hidden,
        ),
        name="experts",
    )(where, *xs, cotangents, cotangents, codes, codes, router, gate_mat, up_mat, down_mat, *kept)
    return results[0:2], results[2:4], results[4:]


def gathered(
    tokens,
    segments,
    prefix,
    expert_ids,
    first_gain,
    query_weight,
    key_matrix,
    value_matrix,
    query_gain,
    key_gain,
    output_weight,
    second_gain,
    router,
    gate_weight,
    up_weight,
    down_weight,
    cotangent,
):
    low = jnp.bfloat16
    full = jnp.float32
    tp_count = lax.axis_size("tp")
    fsdp_count = lax.axis_size("fsdp")
    tp_rank = lax.axis_index("tp")
    fsdp_rank = lax.axis_index("fsdp")
    own_rows, model_dim = tokens.shape
    seq_len = own_rows * tp_count
    head_dim = fsdp_count * query_gain.shape[0]
    query_count = query_weight.shape[1] // head_dim
    kv_count = key_matrix.shape[1] // head_dim
    score_scale = head_dim ** (-0.5)
    local_experts, hidden_units = gate_weight.shape[:2]
    expert_total = fsdp_count * local_experts
    top_count = expert_ids.shape[1]
    capacity = (9 * top_count * seq_len + 8 * expert_total - 1) // (8 * expert_total)

    token_blocks = tp_gather(tokens)
    wide_shard = jnp.concatenate([query_weight, key_matrix, value_matrix], axis=1)
    wide_all = lax.all_gather(wide_shard, "fsdp", axis=0, tiled=True)

    lane_pad = 128
    lanes = jnp.arange(expert_total, dtype=jnp.int32)
    picked = jnp.sum((expert_ids[:, :, None] == lanes[None, None, :]).astype(full), axis=1)
    order = jnp.arange(seq_len, dtype=jnp.int32)
    before = (order[None, :] < order[:, None]).astype(low)
    earlier = jnp.dot(before, picked.astype(low), preferred_element_type=full)
    code = (picked * (1.0 + (earlier < capacity).astype(full))).astype(low)
    small_parts = [first_gain, second_gain, query_gain, key_gain, router.T, code.T]
    small_shard = jnp.concatenate([part.reshape(-1) for part in small_parts])
    small_size = small_shard.shape[0]
    small_shard = jnp.pad(small_shard, (0, -small_size % (16 * lane_pad))).reshape(-1, lane_pad)
    small_all = lax.all_gather(small_shard, "fsdp", axis=0).reshape(fsdp_count, -1)
    taken = []
    begin = 0
    for part in small_parts:
        taken.append(small_all[:, begin : begin + part.size])
        begin += part.size
    gain_one, gain_two, gain_query, gain_key = [part.reshape(-1).astype(full) for part in taken[:4]]
    shift = fsdp_rank * local_experts
    router_near = jnp.swapaxes(taken[4].reshape(fsdp_count, expert_total, -1), 0, 1).reshape(expert_total, model_dim)
    router_near = lax.dynamic_slice_in_dim(
        jnp.concatenate([router_near, router_near], axis=0), shift, expert_total, 0
    )
    router_near = jnp.pad(router_near, ((0, lane_pad - expert_total), (0, 0)))
    codes = taken[5].reshape(fsdp_count, expert_total, seq_len)
    codes = lax.dynamic_slice_in_dim(jnp.concatenate([codes, codes], axis=1), shift, expert_total, 1)
    codes = jnp.pad(jnp.swapaxes(codes, 1, 2), ((0, 0), (0, 0), (0, lane_pad - expert_total)))
    codes = codes.reshape(fsdp_count, tp_count, own_rows, lane_pad)
    output_all = lax.all_gather(output_weight, "fsdp", axis=0, tiled=True)
    cotangent_all = lax.all_gather(cotangent, ("fsdp", "tp"), axis=0, tiled=True)
    cotangent_all = cotangent_all.reshape(fsdp_count, tp_count, own_rows, model_dim)

    segment_row = xor_order(segments[0].reshape(tp_count, own_rows), tp_rank, 0).reshape(-1)
    token_pos = xor_order(order.reshape(tp_count, own_rows), tp_rank, 0).reshape(-1)
    prefix_len = prefix[0]
    doc_start = jnp.sum((segment_row[None, :] < segment_row[:, None]).astype(jnp.int32), axis=1)
    cos_table, sin_table = turned_tables(token_pos - doc_start, head_dim)

    seq_rows = jnp.concatenate(token_blocks, axis=0)
    input_hat, input_inverse = norm_forward(seq_rows.astype(full))
    first_normed = (input_hat * gain_one).astype(low)
    wide_pre = jnp.dot(first_normed, wide_all, preferred_element_type=full)
    query_cols = query_count * head_dim
    kv_cols = kv_count * head_dim
    query_pre = wide_pre[:, :query_cols].reshape(seq_len, query_count, head_dim)
    key_pre = wide_pre[:, query_cols : query_cols + kv_cols].reshape(seq_len, kv_count, head_dim)
    value_heads = wide_pre[:, query_cols + kv_cols :].astype(low).reshape(seq_len, kv_count, head_dim)
    query_hat, query_inverse = norm_forward(query_pre)
    key_hat, key_inverse = norm_forward(key_pre)
    query_heads = rotate(query_hat * gain_query, cos_table, sin_table).astype(low)
    key_heads = rotate(key_hat * gain_key, cos_table, sin_table).astype(low)
    span = min(512, seq_len)
    starts = jnp.arange(seq_len // span, dtype=jnp.int32) * span
    mixed_rows, log_totals = lax.map(
        lambda begin: forward_block(
            begin, query_heads, key_heads, value_heads, segment_row, token_pos, prefix_len, span, score_scale
        ),
        starts,
    )
    mixed_low = mixed_rows.reshape(seq_len, query_cols).astype(low)
    attended_part = jnp.einsum("sa,da->sd", mixed_low, output_all, preferred_element_type=full).astype(low)
    attended = tp_reduce([attended_part[r * own_rows : (r + 1) * own_rows] for r in range(tp_count)])
    hidden = tokens.astype(full) + attended
    hidden_hat, hidden_inverse = norm_forward(hidden)
    normed_two = (hidden_hat * gain_two).astype(low)

    gate_mat = gate_weight.reshape(-1, model_dim)
    up_mat = up_weight.reshape(-1, model_dim)
    down_mat = down_weight.reshape(-1, model_dim)
    core = fsdp_rank % 2
    row_sums, out_terms, kept = [], [], ()
    for r, block in enumerate(tp_gather(normed_two)):
        near = plane_gather(block)
        where = jnp.stack([core, tp_rank ^ r]).astype(jnp.int32)
        row_terms, out_term, kept = expert_call(
            where,
            (near, swap(near, "fsdp", 1)),
            cotangent_all,
            codes,
            router_near,
            gate_mat,
            up_mat,
            down_mat,
            local_experts,
            kept,
        )
        row_sums.append(plane_reduce(row_terms))
        out_terms.append(out_term)
    normed_two_grad = tp_reduce(row_sums)
    out_terms, normed_two_grad = lax.optimization_barrier((out_terms, normed_two_grad))
    output = (hidden + tp_reduce([plane_reduce(term) for term in out_terms])).astype(low)
    normed_all, mixed_all, act_all = [part.reshape(-1, part.shape[-1]) for part in kept]
    wide_grad = jnp.einsum("tf,td->fd", mixed_all, normed_all, preferred_element_type=full)
    down_grad = jnp.einsum(
        "tf,td->fd", act_all, cotangent_all.reshape(-1, model_dim), preferred_element_type=full
    )
    flat_hidden = local_experts * hidden_units
    gate_wgrad = wide_grad[:flat_hidden].reshape(gate_weight.shape)
    up_wgrad = wide_grad[flat_hidden : 2 * flat_hidden].reshape(up_weight.shape)
    down_wgrad = down_grad.reshape(down_weight.shape)
    router_part = wide_grad[2 * flat_hidden : 2 * flat_hidden + expert_total]
    router_part = jnp.concatenate([router_part, router_part], axis=0)
    router_part = lax.dynamic_slice_in_dim(router_part, expert_total - shift, expert_total, 0).T

    hidden_grad = cotangent.astype(full) + norm_back(normed_two_grad, hidden_hat, hidden_inverse, gain_two)
    second_part = jnp.sum(normed_two_grad * hidden_hat, axis=0)
    attended_grad = jnp.concatenate(tp_gather(hidden_grad.astype(low)), axis=0)
    output_wgrad = jnp.einsum("sd,sa->da", attended_grad, mixed_low, preferred_element_type=full)
    mixed_grad = jnp.dot(attended_grad, output_all, preferred_element_type=full).astype(low)
    zero_heads = jnp.zeros((seq_len, kv_count, head_dim), full)
    (key_turn_grad, value_grad), query_turn_grad = lax.scan(
        lambda carried, inputs: backward_block(
            carried,
            inputs,
            query_heads,
            key_heads,
            value_heads,
            mixed_grad,
            segment_row,
            token_pos,
            prefix_len,
            span,
            score_scale,
        ),
        (zero_heads, zero_heads),
        (starts, log_totals),
    )
    query_turn_grad = query_turn_grad.reshape(seq_len, query_count, head_dim)
    query_norm_grad = rotate_back(query_turn_grad, cos_table, sin_table)
    key_norm_grad = rotate_back(key_turn_grad, cos_table, sin_table)
    query_gain_part = jnp.sum(query_norm_grad * query_hat, axis=(0, 1))
    key_gain_part = jnp.sum(key_norm_grad * key_hat, axis=(0, 1))
    query_pre_grad = norm_back(query_norm_grad, query_hat, query_inverse, gain_query).astype(low)
    key_pre_grad = norm_back(key_norm_grad, key_hat, key_inverse, gain_key).astype(low)
    wide_pre_grad = jnp.concatenate(
        [
            query_pre_grad.reshape(seq_len, -1),
            key_pre_grad.reshape(seq_len, -1),
            value_grad.astype(low).reshape(seq_len, -1),
        ],
        axis=1,
    )
    wide_wgrad = jnp.einsum("sd,sa->da", first_normed, wide_pre_grad, preferred_element_type=full)
    normed_one_part = jnp.einsum("sa,da->sd", wide_pre_grad, wide_all, preferred_element_type=full).astype(low)
    normed_one_grad = tp_reduce([normed_one_part[r * own_rows : (r + 1) * own_rows] for r in range(tp_count)])
    own_hat, own_inverse = norm_forward(tokens.astype(full))
    first_part = jnp.sum(normed_one_grad * own_hat, axis=0)
    input_grad = (hidden_grad + norm_back(normed_one_grad, own_hat, own_inverse, gain_one)).astype(low)

    sizes = []
    pieces = []
    for part in (first_part, second_part, query_gain_part, key_gain_part, router_part):
        part = part.reshape(fsdp_count, tp_count, -1)
        sizes.append(part.shape[2])
        pieces.append(part)
    packed = jnp.concatenate(pieces, axis=2)
    packed = small_reduce(xor_order(xor_order(packed, fsdp_rank, 0), tp_rank, 1))
    small = []
    begin = 0
    for size in sizes:
        small.append(packed[begin : begin + size])
        begin += size
    wide_wshard = lax.psum_scatter(wide_wgrad.astype(low), "fsdp", scatter_dimension=0, tiled=True).astype(full)
    output_wshard = lax.psum_scatter(
        output_wgrad.astype(low), "fsdp", scatter_dimension=0, tiled=True
    ).astype(full)
    return (
        output,
        input_grad,
        small[0],
        wide_wshard[:, :query_cols],
        wide_wshard[:, query_cols : query_cols + kv_cols],
        wide_wshard[:, query_cols + kv_cols :],
        small[2],
        small[3],
        output_wshard,
        small[1],
        small[4].reshape(-1, expert_total),
        gate_wgrad,
        up_wgrad,
        down_wgrad,
    )


def solution(mesh):
    placed = (
        P(("fsdp", "tp"), None),
        P("fsdp", None),
        P("fsdp"),
        P("fsdp", None),
        P("fsdp"),
        P("fsdp", "tp"),
        P("fsdp", "tp"),
        P("fsdp", "tp"),
        P("fsdp"),
        P("fsdp"),
        P("fsdp", "tp"),
        P("fsdp"),
        P("fsdp", None),
        P("fsdp", "tp", None),
        P("fsdp", "tp", None),
        P("fsdp", "tp", None),
        P(("fsdp", "tp"), None),
    )
    return jax.shard_map(
        gathered if mesh.shape["fsdp"] == 8 and mesh.shape["tp"] == 4 else exchanged,
        mesh=mesh,
        in_specs=placed,
        out_specs=(
            P(("fsdp", "tp"), None),
            P(("fsdp", "tp"), None),
            P(("fsdp", "tp")),
            P("fsdp", "tp"),
            P("fsdp", "tp"),
            P("fsdp", "tp"),
            P(("fsdp", "tp")),
            P(("fsdp", "tp")),
            P("fsdp", "tp"),
            P(("fsdp", "tp")),
            P(("fsdp", "tp"), None),
            P("fsdp", "tp", None),
            P("fsdp", "tp", None),
            P("fsdp", "tp", None),
        ),
        check_vma=False,
    )
```
